32 devices in a mesh: gx: 4 (over z), gy: 4 (over x, core), gz: 2 (over y).
Axes of the slice: x: 2, y: 2, z: 4, core: 2. Of those that a mesh axis runs over, the one named last changes fastest.
Arguments:
- moving_image: float32 [64, 128, 512], P('gz', 'gx', 'gy'), may hold values from -6 to 6
- fixed_image: float32 [64, 128, 512], P('gz', 'gx', 'gy'), may hold values from -6 to 6
- subvoxel: float32 [3], replicated, may hold values from 0.05 to 0.95
- brick_offset: int32 [2, 8, 32], P(None, 'gx', 'gy'), may hold values from -16 to 16, as said below
Outputs:
- brick_ncc: float32 [8, 32], P('gx', 'gy')
- control_grad: float32 [3, 4, 8, 32], P(None, None, 'gx', 'gy')
The draws below stay inside these ranges and needn't reach their ends.
Inputs may be any that keep to these rules, and one draw needn't show every extreme that they name: `brick_offset`: row 0 of each draw holds both -16 and 16 somewhere, and so does row 1.
All inputs are finite; a program needn't handle non-finite values.
Results may differ from the reference program's by a relative error of at most 0.00023.
Values sent between devices are 32-bit elements; how exact they have to be, the bound alone decides.
A program may use at most 128 MiB of HBM per device.

```python
import jax
import jax.numpy as jnp
from jax import lax

NZ = 64
BRICK = 16
RANGE = 16
NX = 128
NY = 512


def draw_brick_offset(key, part):
    row_count = NX // BRICK
    col_count = NY // BRICK
    values = jax.random.randint(key, (2, row_count, col_count), -RANGE, RANGE + 1, dtype=jnp.int32)
    row_pick = jax.random.randint(jax.random.fold_in(key, 11), (2,), 0, row_count, dtype=jnp.int32)
    col_pick = jax.random.randint(jax.random.fold_in(key, 12), (2,), 0, col_count, dtype=jnp.int32)
    for component in range(2):
        values = values.at[component, row_pick[component], col_pick[component]].set(RANGE)
        values = values.at[component, (row_pick[component] + 1) % row_count, col_pick[component]].set(-RANGE)
    return values


def steps_of(rng, extent, split, low, high):
    factor_of, own = 1.0, jax.random.fold_in(rng, 6)
    for axis_at, shards_of in split:
        draws = jnp.exp(jax.random.uniform(jax.random.fold_in(own, axis_at), (shards_of,), jnp.float32, low / len(split), high / len(split)))
        factor_of = factor_of * jnp.repeat(draws, extent[axis_at] // shards_of).reshape([-1 if axis == axis_at else 1 for axis in range(len(extent))])
    return factor_of


def gaussian(key, shape, scale, limit, shards=(), kind=jnp.bfloat16):
    values = jax.random.normal(key, shape, jnp.float32) * scale
    if len(shards) > 0:
        values = steps_of(key, shape, shards, -0.22, 0.18) * values
    return jnp.clip(values, min=-limit, max=limit).astype(kind)


def setup_inputs(seed: int = 0) -> dict:
    keys = jax.random.split(jax.random.key(seed), 5)
    moving_image = gaussian(keys[0], (NZ, NX, NY), 1.0, 6.0, ((0, 2), (1, 4), (2, 4)), jnp.float32)
    fixed_image = gaussian(keys[1], (NZ, NX, NY), 1.0, 6.0, ((0, 2), (1, 4), (2, 4)), jnp.float32)
    subvoxel = jnp.clip(jax.random.uniform(keys[2], (3,), jnp.float32, 0.05, 0.95), 0.05, 0.95)
    brick_offset = draw_brick_offset(jax.random.fold_in(keys[4], 71), 0)
    return {"moving_image": moving_image, "fixed_image": fixed_image, "subvoxel": subvoxel, "brick_offset": brick_offset}


EPSILON = 1e-06
SUPPORT_NORM = 64.0

def spline_solve(volume, along):
    leading = jnp.moveaxis(volume, along, 0)
    line_len = leading.shape[0]
    flattened = leading.reshape(line_len, -1)
    unit_ones = jnp.ones((line_len,), volume.dtype)
    sub_diag = (unit_ones / 6.0).at[0].set(0.0)
    super_diag = (unit_ones / 6.0).at[line_len - 1].set(0.0)
    solved = lax.linalg.tridiagonal_solve(sub_diag, unit_ones * (4.0 / 6.0), super_diag, flattened)
    return jnp.moveaxis(solved.reshape(leading.shape), 0, along)

def tap_weights(subvoxel):
    shift = subvoxel
    smooth = jnp.stack([(1.0 - shift) ** 3 / 6.0, (3.0 * shift ** 3 - 6.0 * shift ** 2 + 4.0) / 6.0, (-3.0 * shift ** 3 + 3.0 * shift ** 2 + 3.0 * shift + 1.0) / 6.0, shift ** 3 / 6.0])
    slope = jnp.stack([-(1.0 - shift) ** 2 / 2.0, (3.0 * shift ** 2 - 4.0 * shift) / 2.0, (-3.0 * shift ** 2 + 2.0 * shift + 1.0) / 2.0, shift ** 2 / 2.0])
    return (smooth, slope)

def apply_taps(volume, along, weights):
    span_len = volume.shape[along] - 3
    running = weights[0] * lax.slice_in_dim(volume, 0, span_len, axis=along)
    for tap_num in range(1, 4):
        running = running + weights[tap_num] * lax.slice_in_dim(volume, tap_num, tap_num + span_len, axis=along)
    return running

def spread(depth_pair, smooth_x, slope_x, smooth_y, slope_y):
    x_smooth = apply_taps(depth_pair, 2, smooth_x)
    x_slope = apply_taps(depth_pair[0], 1, slope_x)
    value_field = apply_taps(x_smooth[0], 2, smooth_y)
    slope_dz = apply_taps(x_smooth[1], 2, smooth_y)
    slope_dx = apply_taps(x_slope, 2, smooth_y)
    slope_dy = apply_taps(x_smooth[0], 2, slope_y)
    return jnp.stack([value_field, slope_dx, slope_dy, slope_dz])

def resample(fields, brick_offset):
    span_x = fields.shape[2] - 2 * RANGE
    span_y = fields.shape[3] - 2 * RANGE
    shift_x = jnp.repeat(jnp.repeat(brick_offset[0], BRICK, axis=0), BRICK, axis=1)
    shift_y = jnp.repeat(jnp.repeat(brick_offset[1], BRICK, axis=0), BRICK, axis=1)
    source_x = jnp.arange(span_x, dtype=jnp.int32)[:, None] + shift_x + RANGE
    source_y = jnp.arange(span_y, dtype=jnp.int32)[None, :] + shift_y + RANGE
    return fields[:, :, source_x, source_y]

def brick_sums(volume):
    depth_len, width_x, width_y = volume.shape
    return volume.reshape(depth_len, width_x // BRICK, BRICK, width_y // BRICK, BRICK).sum(axis=(0, 2, 4))

def expand(per_brick):
    return jnp.repeat(jnp.repeat(per_brick, BRICK, axis=0), BRICK, axis=1)[None]

def bspline(offset):
    magnitude = jnp.abs(offset)
    inner = 2.0 / 3.0 - magnitude * magnitude + 0.5 * magnitude * magnitude * magnitude
    outer = jnp.maximum(2.0 - magnitude, 0.0) ** 3 / 6.0
    return jnp.where(magnitude < 1.0, inner, outer)

def basis(point_count, first_point, cell_count, first_cell):
    points = first_point + jnp.arange(point_count, dtype=jnp.int32)
    cell_pos = first_cell + jnp.arange(cell_count, dtype=jnp.int32)
    offset = (cell_pos[None, :] - BRICK * points[:, None] - BRICK // 2).astype(jnp.float32) / BRICK
    return bspline(offset)

def reference(moving_image, fixed_image, subvoxel, brick_offset):
    coeffs = spline_solve(spline_solve(spline_solve(moving_image, 1), 2), 0)
    smooth_w, slope_w = tap_weights(subvoxel)
    padded = jnp.pad(coeffs, ((1, 2), (RANGE + 1, RANGE + 2), (RANGE + 1, RANGE + 2)))
    depth_pair = jnp.stack([apply_taps(padded, 0, smooth_w[:, 0]), apply_taps(padded, 0, slope_w[:, 0])])
    fields = spread(depth_pair, smooth_w[:, 1], slope_w[:, 1], smooth_w[:, 2], slope_w[:, 2])
    global_x = jnp.arange(NX + 2 * RANGE, dtype=jnp.int32) - RANGE
    global_y = jnp.arange(NY + 2 * RANGE, dtype=jnp.int32) - RANGE
    inside_x = (global_x >= 0) & (global_x < NX)
    inside_y = (global_y >= 0) & (global_y < NY)
    inside = inside_x[:, None] & inside_y[None, :]
    fields = jnp.where(inside[None, None], fields, 0.0)
    picked = resample(fields, brick_offset)
    warped = picked[0]
    voxel_count = NZ * BRICK * BRICK
    mean_fixed = brick_sums(fixed_image) / voxel_count
    mean_warped = brick_sums(warped) / voxel_count
    centered_f = fixed_image - expand(mean_fixed)
    centered_w = warped - expand(mean_warped)
    fixed_sq = brick_sums(centered_f * centered_f)
    warped_sq = brick_sums(centered_w * centered_w)
    cross_sum = brick_sums(centered_f * centered_w)
    inv_norm = lax.rsqrt(fixed_sq * warped_sq + EPSILON)
    brick_ncc = cross_sum * inv_norm
    slope_ratio = cross_sum / (warped_sq + EPSILON)
    gradient = voxel_count * expand(inv_norm) * (centered_f - expand(slope_ratio) * centered_w)
    forces = gradient[None] * picked[1:4]
    basis_x = basis(NX // BRICK, 0, NX, 0)
    basis_y = basis(NY // BRICK, 0, NY, 0)
    basis_z = basis(NZ // BRICK, 0, NZ, 0)

    def project(component):
        along_y = jnp.dot(component.reshape(-1, NY), basis_y.T, precision=lax.Precision.HIGHEST)
        along_y = along_y.reshape(NZ, NX, NY // BRICK)
        along_x = jnp.einsum('ix,zxj->zij', basis_x, along_y, precision=lax.Precision.HIGHEST)
        return jnp.einsum('kz,zij->kij', basis_z, along_x, precision=lax.Precision.HIGHEST) / SUPPORT_NORM
    control_grad = jnp.stack([project(forces[direction]) for direction in range(3)])
    return (brick_ncc, control_grad)
```

```python
import functools
import math

import jax
import jax.numpy as jnp
import numpy as np
from jax import lax
from jax.experimental import pallas as pl
from jax.experimental.pallas import tpu as pltpu
from jax.sharding import PartitionSpec as P

BRICK = 16
RANGE = 16
EPSILON = 1e-06
SUPPORT_NORM = 64.0
LOG_POLE = math.log(2.0 + math.sqrt(3.0))
POLE = 2.0 - math.sqrt(3.0)
PAD = 32
HALO = RANGE + 2
F32 = jnp.float32
BF16 = jnp.bfloat16
MESH = pl.DeviceIdType.MESH
HIGHEST = lax.Precision.HIGHEST


def factor_table(length):
    t = np.arange(-PAD, length + PAD, dtype=np.float64) + 1.0
    inside = (t >= 1) & (t <= length)
    ti = np.clip(t, 1, length)
    scale = (1.0 / POLE - POLE) * (1.0 - POLE ** (2.0 * (length + 1)))
    low = 1.0 - POLE ** (2.0 * ti)
    high = 1.0 - POLE ** (2.0 * (length + 1 - ti))
    diag = 6.0 * low * high / scale
    fwd = -POLE * high / (1.0 - POLE ** (2.0 * (length + 2 - ti)))
    bwd = -POLE * low / (1.0 - POLE ** (2.0 * (ti + 1)))
    return [np.where(inside, v, 0.0) for v in (diag, fwd, bwd)]


def factor_tables(lengths):
    width = max(lengths) + 2 * PAD
    rows = []
    for length in lengths:
        for row in factor_table(length):
            rows.append(np.pad(row, (0, width - row.shape[0])))
    return np.stack(rows).astype(np.float32).reshape(-1), width


def inverse_entry(row, col, length):
    nearer = jnp.minimum(row, col).astype(F32) + 1.0
    farther = jnp.maximum(row, col).astype(F32) + 1.0
    entry = jnp.exp((nearer - farther) * LOG_POLE) * (1.0 - jnp.exp(-2.0 * LOG_POLE * nearer))
    entry = entry * (1.0 - jnp.exp(-2.0 * LOG_POLE * (length + 1 - farther)))
    entry = entry * (
        6.0 / ((1.0 / POLE - POLE) * (1.0 - math.exp(-2.0 * LOG_POLE * (length + 1))))
    )
    parity = 1.0 - 2.0 * ((row + col) & 1).astype(F32)
    return entry * parity


def iota(shape, dim):
    return lax.broadcasted_iota(jnp.int32, shape, dim)


def split3(left, right):
    left_hi = left.astype(BF16)
    left_lo = (left - left_hi.astype(F32)).astype(BF16)
    lhs = jnp.concatenate([left_hi, left_hi, left_lo], axis=1)
    return jnp.dot(lhs, right, preferred_element_type=F32)


def stack3(right):
    right_hi = right.astype(BF16)
    right_lo = (right - right_hi.astype(F32)).astype(BF16)
    return jnp.concatenate([right_hi, right_lo, right_hi], axis=0)


def bspline(offset):
    magnitude = jnp.abs(offset)
    inner = 2.0 / 3.0 - magnitude * magnitude + 0.5 * magnitude * magnitude * magnitude
    rest = jnp.maximum(2.0 - magnitude, 0.0)
    outer = rest * rest * rest / 6.0
    return jnp.where(magnitude < 1.0, inner, outer)


def taps_of(t):
    smooth = (
        (1.0 - t) * (1.0 - t) * (1.0 - t) / 6.0,
        (3.0 * t * t * t - 6.0 * t * t + 4.0) / 6.0,
        (-3.0 * t * t * t + 3.0 * t * t + 3.0 * t + 1.0) / 6.0,
        t * t * t / 6.0,
    )
    slope = (
        -((1.0 - t) * (1.0 - t)) / 2.0,
        (3.0 * t * t - 4.0 * t) / 2.0,
        (-3.0 * t * t + 2.0 * t + 1.0) / 2.0,
        t * t / 2.0,
    )
    return smooth, slope


def kernel(
    cfg, table, sub, off, img, fix, ncc_out, grad_out,
    uz, zrecv, cz, ux, xl, xr, ce, packl, packr, yl, yr, w0, w1, g0, g1, hs,
    ft, wv, px, py, pz, stat, statr, part, gather,
    s_send, s_recv, f_send, f_recv,
):
    (nx_dev, ny_dev, width_t, nz, nx, ny, dz, dx, dy, zp, ex) = cfg
    me_x, me_y, me_z = (lax.axis_index(a) for a in ("gx", "gy", "gz"))
    other_z = 1 - me_z
    start_x, start_y, start_z = me_x * dx, me_y * dy, me_z * dz
    nbx, nby = dx // BRICK, dy // BRICK

    peers = []
    for ix in (-1, 0, 1):
        for iy in (-1, 0, 1):
            for iz in (0, 1):
                if (ix, iy, iz) == (0, 0, 0):
                    continue
                px_, py_ = me_x + ix, me_y + iy
                ok = (px_ >= 0) & (px_ < nx_dev) & (py_ >= 0) & (py_ < ny_dev)
                target = (px_, py_, other_z if iz else me_z)
                peers.append((ix, iy, iz, ok, target))
    barrier = pltpu.get_barrier_semaphore()
    count = jnp.int32(0)
    for ix, iy, iz, ok, target in peers:
        @pl.when(ok)
        def _(target=target):
            pl.semaphore_signal(barrier, inc=1, device_id=target, device_id_type=MESH)
        count = count + ok.astype(jnp.int32)

    def coef(axis, kind, pos):
        return table[(3 * axis + kind) * width_t + PAD + pos]

    def local_solve(axis, start, length, load, store):
        state = None
        for r in range(length):
            term = coef(axis, 0, start + r) * load(r)
            state = term if state is None else term + coef(axis, 1, start + r) * state
            store(r, state)
        return None

    fwd = []
    state = None
    def zbody(i, state):
        state = coef(0, 0, start_z + i) * img[i] + coef(0, 1, start_z + i) * state
        uz[i] = state
        return state
    lax.fori_loop(0, dz, zbody, jnp.zeros((dx, dy), F32))
    def zback(i, state):
        r = dz - 1 - i
        state = coef(0, 2, start_z + r) * state
        uz[r] = uz[r] + state
        return state + coef(0, 0, start_z + r) * img[r]
    lax.fori_loop(0, dz, zback, jnp.zeros((dx, dy), F32))

    pl.semaphore_wait(barrier, count)
    first = jnp.where(me_z == 0, dz - 2, 0)
    z_copy = pltpu.make_async_remote_copy(
        src_ref=uz.at[pl.ds(first, 2)], dst_ref=zrecv, send_sem=s_send.at[0], recv_sem=s_recv.at[0],
        device_id=(me_x, me_y, other_z), device_id_type=MESH)
    z_copy.start()

    has_l, has_r = me_x > 0, me_x < nx_dev - 1
    has_d, has_u = me_y > 0, me_y < ny_dev - 1
    for have, ref in ((has_l, xl), (has_r, xr), (has_d, yl), (has_u, yr)):
        @pl.when(jnp.logical_not(have))
        def _(ref=ref):
            ref[...] = jnp.zeros(ref.shape, F32)

    tz, sz = taps_of(sub[0])
    tx, sx = taps_of(sub[1])
    ty, sy = taps_of(sub[2])
    lane = iota((1, dy), 1)
    group = lane // BRICK
    ox_v, oy_v = [], []
    for bx in range(nbx):
        vx = jnp.zeros((1, dy), jnp.int32)
        vy = jnp.zeros((1, dy), jnp.int32)
        for by in range(nby):
            vx = jnp.where(group == by, off[0, bx, by], vx)
            vy = jnp.where(group == by, off[1, bx, by], vy)
        ox_v.append(vx)
        oy_v.append(vy)

    nslot = dy // HALO
    col = iota((dy, 2 * dy), 1)
    src = iota((dy, 2 * dy), 0)
    lane_in = jnp.where(col < dy, col, col - dy)
    slot = lane_in // HALO
    at = lane_in - slot * HALO + jnp.where(col < dy, 0, dy - HALO)
    ends = jnp.where(slot < nslot, inverse_entry(start_y + at, start_y + src, ny), 0.0)

    wide = 2 * dy
    jcol = iota((dy, wide), 1) - HALO
    jin = (start_y + jcol >= 0) & (start_y + jcol < ny) & (jcol < dy + HALO)
    own_part = jnp.where(jin, inverse_entry(
        jnp.clip(start_y + jcol, 0, ny - 1), start_y + iota((dy, wide), 0), ny), 0.0)
    m = iota((dy, wide), 0)
    jf = (start_y + jcol + 1).astype(F32)
    parity = 1.0 - 2.0 * (jcol & 1).astype(F32)
    t_left = (start_y * jnp.ones((1, 1), jnp.int32)).astype(F32)
    t_right = t_left + float(dy + 1)
    high = 1.0 - jnp.exp(-2.0 * LOG_POLE * (ny + 1 - jf))
    low = 1.0 - jnp.exp(-2.0 * LOG_POLE * jf)
    jown = jcol.astype(F32)
    from_left = -parity * jnp.exp(-LOG_POLE * (jown + 1.0)) * high / (
        1.0 - jnp.exp(-2.0 * LOG_POLE * (ny + 1 - t_left)))
    from_right = parity * jnp.exp(LOG_POLE * (jown - float(dy))) * low / (
        1.0 - jnp.exp(-2.0 * LOG_POLE * t_right))
    if dy % 2:
        from_right = -from_right
    left_col = jnp.where(jcol < 0, jnp.where(m - HALO == jcol, 1.0, 0.0),
                         jnp.where(m == HALO - 1, from_left, 0.0))
    right_col = jnp.where(jcol >= dy, jnp.where(m - HALO + dy == jcol, 1.0, 0.0),
                          jnp.where(m == HALO, from_right, 0.0))
    halo_part = jnp.where(m < HALO, left_col, jnp.where(m < 2 * HALO, right_col, 0.0))
    halo_part = jnp.where(jin, halo_part, 0.0)
    full_y = jnp.concatenate([own_part, halo_part], axis=0)
    for bx, wref in ((0, w0), (1, w1)):
        jrow = iota((wide, dy), 0) - HALO
        want = lane + oy_v[bx]
        ok_y = jnp.where((start_y + want >= 0) & (start_y + want < ny), 1.0, 0.0)
        picks = []
        for taps in (ty, sy):
            acc = jnp.zeros((wide, dy), F32)
            for c in range(4):
                acc = jnp.where(jrow == want + (c - 1), taps[c], acc)
            picks.append(acc * ok_y)
        wref[...] = stack3(jnp.dot(full_y, jnp.concatenate(picks, axis=1), precision=HIGHEST,
                                   preferred_element_type=F32))

    ones = jnp.where(iota((dy, dy), 0) // BRICK == iota((dy, dy), 1) // BRICK, 1.0, 0.0)
    half = float(dz * BRICK * BRICK)

    def group_sum(rows):
        return jnp.dot(rows, ones, precision=HIGHEST, preferred_element_type=F32)

    def row8(vecs):
        rows = iota((8, dy), 0)
        out = jnp.zeros((8, dy), F32)
        for i, v in enumerate(vecs):
            out = jnp.where(rows == i, v, out)
        return out

    for i in range(dx // 8):
        ft[8 * i:8 * i + 8] = jnp.swapaxes(fix[:, 8 * i:8 * i + 8, :], 0, 1)
    fsum = [jnp.sum(jnp.sum(ft[BRICK * b:BRICK * b + BRICK], axis=0), axis=0, keepdims=True) for b in range(nbx)]
    mean_f = group_sum(row8(fsum)) / half
    sff = []
    for b in range(nbx):
        cf = ft[BRICK * b:BRICK * b + BRICK] - mean_f[b:b + 1][None]
        ft[BRICK * b:BRICK * b + BRICK] = cf
        sff.append(jnp.sum(jnp.sum(cf * cf, axis=0), axis=0, keepdims=True))

    z_copy.wait()
    left_on = jnp.where(me_z == 1, 1.0, 0.0)
    right_on = 1.0 - left_on
    zl = zrecv[1] * left_on
    zr0, zr1 = zrecv[0] * right_on, zrecv[1] * right_on
    def zf(i, y):
        y = coef(0, 1, start_z + i) * y
        cz[i + 1] = uz[i] + y
        return y
    lax.fori_loop(0, dz, zf, zl)
    y = coef(0, 1, start_z + dz) * cz[dz]
    cz[dz + 1] = zr0 + y
    y = coef(0, 1, start_z + dz + 1) * y
    cz[dz + 2] = zr1 + y
    def zb(i, y):
        r = dz - 1 - i
        y = coef(0, 2, start_z + r) * y
        cz[r + 1] = cz[r + 1] + y
        return y
    y = lax.fori_loop(0, dz, zb, zr0)
    cz[0] = zl + coef(0, 2, start_z - 1) * (uz[0] + y)
    for i in range(dz + 3, zp):
        cz[i] = jnp.zeros((dx, dy), F32)
    for i in range(dx // 8):
        ce[HALO - 1 + 8 * i:HALO - 1 + 8 * i + 8] = jnp.swapaxes(cz[:, 8 * i:8 * i + 8, :], 0, 1)

    def xf(i, y):
        y = coef(1, 0, start_x + i) * ce[HALO - 1 + i] + coef(1, 1, start_x + i) * y
        ux[i] = y
        return y
    lax.fori_loop(0, dx, xf, jnp.zeros((zp, dy), F32))
    def xb(i, y):
        r = dx - 1 - i
        y = coef(1, 2, start_x + r) * y
        ux[r] = ux[r] + y
        return y + coef(1, 0, start_x + r) * ce[HALO - 1 + r]
    lax.fori_loop(0, dx, xb, jnp.zeros((zp, dy), F32))

    def pair(low_src, low_dst, high_src, high_dst, sem, low_id, high_id, low_ok, high_ok):
        low = pltpu.make_async_remote_copy(
            src_ref=low_src, dst_ref=low_dst, send_sem=s_send.at[sem], recv_sem=s_recv.at[sem],
            device_id=low_id, device_id_type=MESH)
        high = pltpu.make_async_remote_copy(
            src_ref=high_src, dst_ref=high_dst, send_sem=s_send.at[sem + 1], recv_sem=s_recv.at[sem + 1],
            device_id=high_id, device_id_type=MESH)
        @pl.when(low_ok)
        def _():
            low.start()
        @pl.when(high_ok)
        def _():
            high.start()
        def wait():
            @pl.when(low_ok)
            def _():
                low.wait_send()
                high.wait_recv()
            @pl.when(high_ok)
            def _():
                high.wait_send()
                low.wait_recv()
        return wait

    wait_x = pair(ux.at[pl.ds(0, HALO)], xr, ux.at[pl.ds(dx - HALO, HALO)], xl, 1,
                  (me_x - 1, me_y, me_z), (me_x + 1, me_y, me_z), has_l, has_r)
    wait_x()
    def gf(i, y):
        y = coef(1, 1, start_x + i) * y
        ce[HALO - 1 + i] = ux[i] + y
        return y
    lax.fori_loop(0, dx, gf, xl[HALO - 1])
    def gr(i, y):
        y = coef(1, 1, start_x + dx + i) * y
        ce[HALO - 1 + dx + i] = xr[i] + y
        return y
    lax.fori_loop(0, HALO, gr, ce[HALO - 1 + dx - 1])
    def gb(i, y):
        r = dx - 1 - i
        y = coef(1, 2, start_x + r) * y
        ce[HALO - 1 + r] = ce[HALO - 1 + r] + y
        return y
    y = lax.fori_loop(0, dx, gb, xr[0])
    def gl(i, y):
        y = coef(1, 2, start_x - 1 - i) * y
        ce[HALO - 2 - i] = xl[HALO - 1 - i] + y
        return y
    lax.fori_loop(0, HALO - 1, gl, ux[0] + y)
    for i in range(dx + 2 * HALO - 1, ex):
        ce[i] = jnp.zeros((zp, dy), F32)

    rows = ex // nslot
    acc = jnp.zeros((rows * zp, 2 * dy), F32)
    for k in range(nslot):
        right = stack3(jnp.where(slot == k, ends, 0.0))
        acc = acc + split3(ce[rows * k:rows * k + rows].reshape(rows * zp, dy), right)
    packl[...] = acc[:, :dy].reshape(rows, zp, dy)
    packr[...] = acc[:, dy:].reshape(rows, zp, dy)
    wait_y = pair(packl, yr, packr, yl, 3,
                  (me_x, me_y - 1, me_z), (me_x, me_y + 1, me_z), has_d, has_u)
    wait_y()

    lane3 = iota((rows * zp, dy), 1)
    for k in range(nslot):
        own = ce[rows * k:rows * k + rows].reshape(rows * zp, dy)
        a = yl[...].reshape(rows * zp, dy)
        b = yr[...].reshape(rows * zp, dy)
        if k > 0:
            a = pltpu.roll(a, dy - HALO * k, 1)
        if k != 1:
            b = pltpu.roll(b, (dy + HALO - HALO * k) % dy, 1)
        halo = jnp.where(lane3 < HALO, a, jnp.where(lane3 < 2 * HALO, b, 0.0))
        both = jnp.concatenate([own, halo], axis=1)
        if k < nslot - 1:
            g0[rows * k:rows * k + rows] = split3(both, w0[...]).reshape(rows, zp, 2 * dy)
        if k > 0:
            g1[rows * (k - 1):rows * k] = split3(both, w1[...]).reshape(rows, zp, 2 * dy)

    group2 = jnp.concatenate([group, group], axis=1)
    wsum = []
    for bx, gref in ((0, g0), (1, g1)):
        base = [off[0, bx, by] + RANGE + bx * (BRICK - rows) for by in range(nby)]
        def pick(i, c, gref=gref, base=base):
            v = gref[base[0] + i]
            for by in range(1, nby):
                v = jnp.where(group2 == by, gref[base[by] + i], v)
            hs[i] = v
            return c
        lax.fori_loop(0, BRICK + 3, pick, 0)
        def fir(i, total, bx=bx):
            gx_pos = start_x + bx * BRICK + i + ox_v[bx]
            ok_x = jnp.where((gx_pos >= 0) & (gx_pos < nx), 1.0, 0.0)
            h = [hs[i + c] for c in range(4)]
            hv = [v[:, :dy] for v in h]
            hd = [v[:, dy:] for v in h]
            def comb(w, vs):
                return (w[0] * vs[0] + w[1] * vs[1] + w[2] * vs[2] + w[3] * vs[3]) * ok_x
            val, dxx, dyy = comb(tx, hv), comb(sx, hv), comb(tx, hd)
            def zfir(w, v):
                return w[0] * v[0:dz] + w[1] * v[1:dz + 1] + w[2] * v[2:dz + 2] + w[3] * v[3:dz + 3]
            out = zfir(tz, val)
            r = bx * BRICK + i
            wv[r] = out
            px[r] = zfir(tz, dxx)
            py[r] = zfir(tz, dyy)
            pz[r] = zfir(sz, val)
            return total + out
        total = lax.fori_loop(0, BRICK, fir, jnp.zeros((dz, dy), F32))
        wsum.append(jnp.sum(total, axis=0, keepdims=True))

    mean_w = group_sum(row8(wsum)) / half
    sww, sfw = [], []
    for b in range(nbx):
        cw = wv[BRICK * b:BRICK * b + BRICK] - mean_w[b:b + 1][None]
        wv[BRICK * b:BRICK * b + BRICK] = cw
        cf = ft[BRICK * b:BRICK * b + BRICK]
        sww.append(jnp.sum(jnp.sum(cw * cw, axis=0), axis=0, keepdims=True))
        sfw.append(jnp.sum(jnp.sum(cf * cw, axis=0), axis=0, keepdims=True))
    sums = group_sum(row8(sff + sww + sfw))
    stat[0] = row8([mean_f[b:b + 1] for b in range(nbx)] + [mean_w[b:b + 1] for b in range(nbx)])
    stat[1] = sums
    st_copy = pltpu.make_async_remote_copy(
        src_ref=stat, dst_ref=statr, send_sem=s_send.at[5], recv_sem=s_recv.at[5],
        device_id=(me_x, me_y, other_z), device_id_type=MESH)
    st_copy.start()
    st_copy.wait()
    voxels = 2.0 * half
    alphas, betas, gammas, nccs = [], [], [], []
    own_m, oth_m = stat[0], statr[0]
    own_s, oth_s = stat[1], statr[1]
    diff = own_m - oth_m
    for b in range(nbx):
        df, dw = diff[b:b + 1], diff[nbx + b:nbx + b + 1]
        def both_halves(i, extra):
            return own_s[i:i + 1] + oth_s[i:i + 1] + extra * (half / 2.0)
        ff = both_halves(b, df * df)
        ww = both_halves(nbx + b, dw * dw)
        fw = both_halves(2 * nbx + b, df * dw)
        inv = lax.rsqrt(ff * ww + EPSILON)
        ratio = fw / (ww + EPSILON)
        nccs.append(fw * inv)
        alphas.append(voxels * inv)
        betas.append(ratio)
        gammas.append(0.5 * (df - ratio * dw))
    every = jnp.where(iota((dy, dy), 0) == BRICK * iota((dy, dy), 1), 1.0, 0.0)
    ncc_rows = jnp.dot(row8(nccs), every, precision=HIGHEST, preferred_element_type=F32)
    ncc_out[...] = ncc_rows[:nbx, :nby]

    zrow = (start_z + iota((dz, 1), 0)).astype(F32)
    bz = [bspline((zrow - float(BRICK * k + BRICK // 2)) / BRICK) for k in range(nz // BRICK)]
    nk = nz // BRICK
    ne = nbx + 4
    ycol = iota((dy, dy), 1)
    yoff = (iota((dy, dy), 0) - BRICK * (ycol - 2) - BRICK // 2).astype(F32) / BRICK
    by_mat = jnp.where(ycol < nby + 4, bspline(yoff), 0.0)
    xrow = [[0.0] * dx for _ in range(ne)]
    for e in range(ne):
        for r in range(dx):
            u = abs(r - BRICK * (e - 2) - BRICK // 2) / BRICK
            xrow[e][r] = (2.0 / 3.0 - u * u + u ** 3 / 2.0) if u < 1 else max(2.0 - u, 0.0) ** 3 / 6.0
    for d, pref in enumerate((px, py, pz)):
        accs = [None] * ne
        for r in range(dx):
            b = r // BRICK
            g = alphas[b] * (ft[r] - betas[b] * wv[r] + gammas[b])
            force = g * pref[r]
            for e in range(ne):
                if xrow[e][r] != 0.0:
                    t = xrow[e][r] * force
                    accs[e] = t if accs[e] is None else accs[e] + t
        for e in range(ne):
            for k in range(nk):
                part[e, d * nk + k:d * nk + k + 1, :] = jnp.sum(accs[e] * bz[k], axis=0, keepdims=True)
    for e in range(ne):
        part[e, 3 * nk:] = jnp.zeros((part.shape[1] - 3 * nk, dy), F32)
    depth = part.shape[1]
    full = jnp.dot(part[...].reshape(ne * depth, dy), by_mat, precision=HIGHEST,
                   preferred_element_type=F32) * (1.0 / SUPPORT_NORM)
    part[...] = full.reshape(ne, depth, dy)

    def slot_of(ix, iy, iz):
        return ((ix + 1) * 3 + (iy + 1)) * 2 + iz

    for ix, iy, iz, ok, target in peers:
        there = slot_of(-ix, -iy, iz)
        here = slot_of(ix, iy, iz)
        @pl.when(jnp.logical_not(ok))
        def _(here=here):
            gather[here] = jnp.zeros(gather.shape[1:], F32)
        @pl.when(ok)
        def _(ix=ix, there=there, target=target):
            pltpu.make_async_remote_copy(
                src_ref=part.at[pl.ds(2 + nbx * ix if ix >= 0 else 0, nbx)] if nbx == 2 else None,
                dst_ref=gather.at[there], send_sem=f_send.at[there], recv_sem=f_recv.at[there],
                device_id=target, device_id_type=MESH).start()
    for ix, iy, iz, ok, target in peers:
        there = slot_of(-ix, -iy, iz)
        here = slot_of(ix, iy, iz)
        @pl.when(ok)
        def _(ix=ix, there=there, here=here, target=target):
            pltpu.make_async_remote_copy(
                src_ref=part.at[pl.ds(2 + nbx * ix if ix >= 0 else 0, nbx)],
                dst_ref=gather.at[there], send_sem=f_send.at[there], recv_sem=f_recv.at[there],
                device_id=target, device_id_type=MESH).wait_send()
            pltpu.make_async_remote_copy(
                src_ref=part.at[pl.ds(0, nbx)],
                dst_ref=gather.at[here], send_sem=f_send.at[here], recv_sem=f_recv.at[here],
                device_id=target, device_id_type=MESH).wait_recv()
    gather_own = part[2:2 + nbx]
    lane_c = iota((nbx * depth, dy), 1)
    result = None
    for iy in (-1, 0, 1):
        total = gather_own if iy == 0 else None
        for ix in (-1, 0, 1):
            for iz in (0, 1):
                if (ix, iy, iz) == (0, 0, 0):
                    continue
                v = gather[slot_of(ix, iy, iz)]
                total = v if total is None else total + v
        total = total.reshape(nbx * depth, dy)
        if iy == 0:
            moved = pltpu.roll(total, dy - 2, 1)
        elif iy < 0:
            moved = jnp.where(lane_c < 2, pltpu.roll(total, dy - (nby + 2), 1), 0.0)
        else:
            moved = jnp.where(lane_c >= nby - 2, pltpu.roll(total, nby - 2, 1), 0.0)
        result = moved if result is None else result + moved
    for i in range(nbx):
        for d in range(3):
            for k in range(nk):
                row = i * depth + d * nk + k
                grad_out[d, k, i:i + 1, :] = result[row:row + 1, :nby]


def shards(sizes, moving_image, fixed_image, subvoxel, brick_offset):
    nx_dev, ny_dev, nz_dev = sizes
    dz, dx, dy = moving_image.shape
    nz, nx, ny = dz * nz_dev, dx * nx_dev, dy * ny_dev
    table, width_t = factor_tables((nz, nx, ny))
    zp = -(-(dz + 3) // 8) * 8
    nslot = dy // HALO
    ex = -(-(dx + 2 * HALO - 1) // nslot) * nslot
    rows = ex // nslot
    nbx, nby, nk = dx // BRICK, dy // BRICK, nz // BRICK
    depth = -(-3 * nk // 8) * 8
    cfg = (nx_dev, ny_dev, width_t, nz, nx, ny, dz, dx, dy, zp, ex)
    vm = lambda *shape: pltpu.VMEM(shape, F32)
    vspec = pl.BlockSpec(memory_space=pltpu.VMEM)
    sspec = pl.BlockSpec(memory_space=pltpu.SMEM)
    return pl.pallas_call(
        functools.partial(kernel, cfg),
        out_shape=(
            jax.ShapeDtypeStruct((nbx, nby), F32),
            jax.ShapeDtypeStruct((3, nk, nbx, nby), F32),
        ),
        in_specs=[sspec, sspec, sspec, vspec, vspec],
        out_specs=(vspec, vspec),
        scratch_shapes=[
            vm(dz, dx, dy), vm(2, dx, dy), vm(zp, dx, dy),
            vm(dx, zp, dy), vm(HALO, zp, dy), vm(HALO, zp, dy), vm(ex, zp, dy),
            vm(rows, zp, dy), vm(rows, zp, dy), vm(rows, zp, dy), vm(rows, zp, dy),
            pltpu.VMEM((6 * dy, 2 * dy), BF16), pltpu.VMEM((6 * dy, 2 * dy), BF16),
            vm(ex - rows, zp, 2 * dy), vm(ex - rows, zp, 2 * dy), vm(BRICK + 3, zp, 2 * dy),
            vm(dx, dz, dy), vm(dx, dz, dy), vm(dx, dz, dy), vm(dx, dz, dy), vm(dx, dz, dy),
            vm(2, 8, dy), vm(2, 8, dy),
            vm(nbx + 4, depth, dy), vm(18, nbx, depth, dy),
            pltpu.SemaphoreType.DMA((6,)), pltpu.SemaphoreType.DMA((6,)),
            pltpu.SemaphoreType.DMA((18,)), pltpu.SemaphoreType.DMA((18,)),
        ],
        compiler_params=pltpu.CompilerParams(
            collective_id=0, has_side_effects=True, vmem_limit_bytes=56 * 1024 * 1024),
    )(jnp.asarray(table), subvoxel, brick_offset, moving_image, fixed_image)


def solution(mesh):
    sizes = (mesh.shape["gx"], mesh.shape["gy"], mesh.shape["gz"])
    return jax.shard_map(
        functools.partial(shards, sizes),
        mesh=mesh,
        in_specs=(P("gz", "gx", "gy"), P("gz", "gx", "gy"), P(), P(None, "gx", "gy")),
        out_specs=(P("gx", "gy"), P(None, None, "gx", "gy")),
        check_vma=False,
    )
```

```python
import functools
import math

import jax
import jax.numpy as jnp
import numpy as np
from jax import lax
from jax.experimental import pallas as pl
from jax.experimental.pallas import tpu as pltpu
from jax.sharding import PartitionSpec as P

BRICK = 16
RANGE = 16
EPSILON = 1e-06
SUPPORT_NORM = 64.0
LOG_POLE = math.log(2.0 + math.sqrt(3.0))
POLE = 2.0 - math.sqrt(3.0)
PAD = 32
HALO = RANGE + 2
F32 = jnp.float32
BF16 = jnp.bfloat16
MESH = pl.DeviceIdType.MESH
HIGHEST = lax.Precision.HIGHEST


def factor_table(length):
    t = np.arange(-PAD, length + PAD, dtype=np.float64) + 1.0
    inside = (t >= 1) & (t <= length)
    ti = np.clip(t, 1, length)
    scale = (1.0 / POLE - POLE) * (1.0 - POLE ** (2.0 * (length + 1)))
    low = 1.0 - POLE ** (2.0 * ti)
    high = 1.0 - POLE ** (2.0 * (length + 1 - ti))
    diag = 6.0 * low * high / scale
    fwd = -POLE * high / (1.0 - POLE ** (2.0 * (length + 2 - ti)))
    bwd = -POLE * low / (1.0 - POLE ** (2.0 * (ti + 1)))
    return [np.where(inside, v, 0.0) for v in (diag, fwd, bwd)]


def factor_tables(lengths):
    width = max(lengths) + 2 * PAD
    rows = []
    for length in lengths:
        for row in factor_table(length):
            rows.append(np.pad(row, (0, width - row.shape[0])))
    return np.stack(rows).astype(np.float32).reshape(-1), width


def inverse_entry(row, col, length):
    nearer = jnp.minimum(row, col).astype(F32) + 1.0
    farther = jnp.maximum(row, col).astype(F32) + 1.0
    entry = jnp.exp((nearer - farther) * LOG_POLE) * (1.0 - jnp.exp(-2.0 * LOG_POLE * nearer))
    entry = entry * (1.0 - jnp.exp(-2.0 * LOG_POLE * (length + 1 - farther)))
    entry = entry * (
        6.0 / ((1.0 / POLE - POLE) * (1.0 - math.exp(-2.0 * LOG_POLE * (length + 1))))
    )
    parity = 1.0 - 2.0 * ((row + col) & 1).astype(F32)
    return entry * parity


def iota(shape, dim):
    return lax.broadcasted_iota(jnp.int32, shape, dim)


def split3(left, right):
    left_hi = left.astype(BF16)
    left_lo = (left - left_hi.astype(F32)).astype(BF16)
    lhs = jnp.concatenate([left_hi, left_hi, left_lo], axis=1)
    return jnp.dot(lhs, right, preferred_element_type=F32)


def stack3(right):
    right_hi = right.astype(BF16)
    right_lo = (right - right_hi.astype(F32)).astype(BF16)
    return jnp.concatenate([right_hi, right_lo, right_hi], axis=0)


def bspline(offset):
    magnitude = jnp.abs(offset)
    inner = 2.0 / 3.0 - magnitude * magnitude + 0.5 * magnitude * magnitude * magnitude
    rest = jnp.maximum(2.0 - magnitude, 0.0)
    outer = rest * rest * rest / 6.0
    return jnp.where(magnitude < 1.0, inner, outer)


def taps_of(t):
    smooth = (
        (1.0 - t) * (1.0 - t) * (1.0 - t) / 6.0,
        (3.0 * t * t * t - 6.0 * t * t + 4.0) / 6.0,
        (-3.0 * t * t * t + 3.0 * t * t + 3.0 * t + 1.0) / 6.0,
        t * t * t / 6.0,
    )
    slope = (
        -((1.0 - t) * (1.0 - t)) / 2.0,
        (3.0 * t * t - 4.0 * t) / 2.0,
        (-3.0 * t * t + 2.0 * t + 1.0) / 2.0,
        t * t / 2.0,
    )
    return smooth, slope


def kernel(
    cfg, table, sub, off, img_hbm, fix_hbm, ncc_out, grad_out,
    img, fix, in_sem, uz, zrecv, cz, ux, xl, xr, ce, packl, packr, yl, yr, ends3, w0, w1, g0, g1, hs,
    ft, wv, px, py, pz, proj, stat, statr, part, gather,
    s_send, s_recv, f_send, f_recv,
):
    (nx_dev, ny_dev, width_t, nz, nx, ny, dz, dx, dy, zp, ex) = cfg
    me_x, me_y, me_z = (lax.axis_index(a) for a in ("gx", "gy", "gz"))
    other_z = 1 - me_z
    start_x, start_y, start_z = me_x * dx, me_y * dy, me_z * dz
    nbx, nby = dx // BRICK, dy // BRICK

    load_img = pltpu.make_async_copy(img_hbm, img, in_sem.at[0])
    load_fix = pltpu.make_async_copy(fix_hbm, fix, in_sem.at[1])
    load_img.start()
    load_fix.start()

    peers = []
    for ix in (-1, 0, 1):
        for iy in (-1, 0, 1):
            for iz in (0, 1):
                if (ix, iy, iz) == (0, 0, 0):
                    continue
                px_, py_ = me_x + ix, me_y + iy
                ok = (px_ >= 0) & (px_ < nx_dev) & (py_ >= 0) & (py_ < ny_dev)
                target = (px_, py_, other_z if iz else me_z)
                peers.append((ix, iy, iz, ok, target))
    barrier = pltpu.get_barrier_semaphore()
    count = jnp.int32(0)
    for ix, iy, iz, ok, target in peers:
        if abs(ix) + abs(iy) + iz > 1:
            continue
        @pl.when(ok)
        def _(target=target):
            pl.semaphore_signal(barrier, inc=1, device_id=target, device_id_type=MESH)
        count = count + ok.astype(jnp.int32)

    def coef(axis, kind, pos):
        return table[(3 * axis + kind) * width_t + PAD + pos]

    load_img.wait()
    def zbody(i, state):
        state = coef(0, 0, start_z + i) * img[i] + coef(0, 1, start_z + i) * state
        uz[i] = state
        return state
    lax.fori_loop(0, dz, zbody, jnp.zeros((dx, dy), F32), unroll=True)
    def zback(i, state):
        r = dz - 1 - i
        state = coef(0, 2, start_z + r) * state
        uz[r] = uz[r] + state
        return state + coef(0, 0, start_z + r) * img[r]
    lax.fori_loop(0, dz, zback, jnp.zeros((dx, dy), F32), unroll=True)

    pl.semaphore_wait(barrier, count)
    first = jnp.where(me_z == 0, dz - 2, 0)
    z_copy = pltpu.make_async_remote_copy(
        src_ref=uz.at[pl.ds(first, 2)], dst_ref=zrecv, send_sem=s_send.at[0], recv_sem=s_recv.at[0],
        device_id=(me_x, me_y, other_z), device_id_type=MESH)
    z_copy.start()

    has_l, has_r = me_x > 0, me_x < nx_dev - 1
    has_d, has_u = me_y > 0, me_y < ny_dev - 1
    for have, ref in ((has_l, xl), (has_r, xr), (has_d, yl), (has_u, yr)):
        @pl.when(jnp.logical_not(have))
        def _(ref=ref):
            ref[...] = jnp.zeros(ref.shape, F32)

    tz, sz = taps_of(sub[0])
    tx, sx = taps_of(sub[1])
    ty, sy = taps_of(sub[2])
    lane = iota((1, dy), 1)
    group = lane // BRICK
    ox_v, oy_v = [], []
    for bx in range(nbx):
        vx = jnp.zeros((1, dy), jnp.int32)
        vy = jnp.zeros((1, dy), jnp.int32)
        for by in range(nby):
            vx = jnp.where(group == by, off[0, bx, by], vx)
            vy = jnp.where(group == by, off[1, bx, by], vy)
        ox_v.append(vx)
        oy_v.append(vy)

    nslot = dy // HALO
    col = iota((dy, 2 * dy), 1)
    src = iota((dy, 2 * dy), 0)
    lane_in = jnp.where(col < dy, col, col - dy)
    slot = lane_in // HALO
    at = lane_in - slot * HALO + jnp.where(col < dy, 0, dy - HALO)
    ends3[...] = stack3(jnp.where(slot == 0, inverse_entry(start_y + at, start_y + src, ny), 0.0))

    wide = 2 * dy
    jcol = iota((dy, wide), 1) - HALO
    jin = (start_y + jcol >= 0) & (start_y + jcol < ny) & (jcol < dy + HALO)
    own_part = jnp.where(jin, inverse_entry(
        jnp.clip(start_y + jcol, 0, ny - 1), start_y + iota((dy, wide), 0), ny), 0.0)
    m = iota((dy, wide), 0)
    jf = (start_y + jcol + 1).astype(F32)
    parity = 1.0 - 2.0 * (jcol & 1).astype(F32)
    t_left = (start_y * jnp.ones((1, 1), jnp.int32)).astype(F32)
    t_right = t_left + float(dy + 1)
    high = 1.0 - jnp.exp(-2.0 * LOG_POLE * (ny + 1 - jf))
    low = 1.0 - jnp.exp(-2.0 * LOG_POLE * jf)
    jown = jcol.astype(F32)
    from_left = -parity * jnp.exp(-LOG_POLE * (jown + 1.0)) * high / (
        1.0 - jnp.exp(-2.0 * LOG_POLE * (ny + 1 - t_left)))
    from_right = parity * jnp.exp(LOG_POLE * (jown - float(dy))) * low / (
        1.0 - jnp.exp(-2.0 * LOG_POLE * t_right))
    if dy % 2:
        from_right = -from_right
    left_col = jnp.where(jcol < 0, jnp.where(m - HALO == jcol, 1.0, 0.0),
                         jnp.where(m == HALO - 1, from_left, 0.0))
    right_col = jnp.where(jcol >= dy, jnp.where(m - HALO + dy == jcol, 1.0, 0.0),
                          jnp.where(m == HALO, from_right, 0.0))
    halo_part = jnp.where(m < HALO, left_col, jnp.where(m < 2 * HALO, right_col, 0.0))
    halo_part = jnp.where(jin, halo_part, 0.0)
    full_y = jnp.concatenate([own_part, halo_part], axis=0)
    for bx, wref in ((0, w0), (1, w1)):
        jrow = iota((wide, dy), 0) - HALO
        want = lane + oy_v[bx]
        ok_y = jnp.where((start_y + want >= 0) & (start_y + want < ny), 1.0, 0.0)
        picks = []
        for taps in (ty, sy):
            acc = jnp.zeros((wide, dy), F32)
            for c in range(4):
                acc = jnp.where(jrow == want + (c - 1), taps[c], acc)
            picks.append(acc * ok_y)
        wref[...] = stack3(jnp.dot(full_y, jnp.concatenate(picks, axis=1), precision=HIGHEST,
                                   preferred_element_type=F32))

    ones = jnp.where(iota((dy, dy), 0) // BRICK == iota((dy, dy), 1) // BRICK, 1.0, 0.0)
    half = float(dz * BRICK * BRICK)

    def group_sum(rows):
        return jnp.dot(rows, ones, precision=HIGHEST, preferred_element_type=F32)

    def row8(vecs):
        rows = iota((8, dy), 0)
        out = jnp.zeros((8, dy), F32)
        for i, v in enumerate(vecs):
            out = jnp.where(rows == i, v, out)
        return out

    load_fix.wait()
    for i in range(dx // 8):
        ft[8 * i:8 * i + 8] = jnp.swapaxes(fix[:, 8 * i:8 * i + 8, :], 0, 1)
    fsum = [jnp.sum(jnp.sum(ft[BRICK * b:BRICK * b + BRICK], axis=0), axis=0, keepdims=True) for b in range(nbx)]
    mean_f = group_sum(row8(fsum)) / half
    sff = []
    for b in range(nbx):
        cf = ft[BRICK * b:BRICK * b + BRICK] - mean_f[b:b + 1][None]
        ft[BRICK * b:BRICK * b + BRICK] = cf
        sff.append(jnp.sum(jnp.sum(cf * cf, axis=0), axis=0, keepdims=True))

    z_copy.wait()
    left_on = jnp.where(me_z == 1, 1.0, 0.0)
    right_on = 1.0 - left_on
    zl = zrecv[1] * left_on
    zr0, zr1 = zrecv[0] * right_on, zrecv[1] * right_on
    def zf(i, y):
        y = coef(0, 1, start_z + i) * y
        cz[i + 1] = uz[i] + y
        return y
    lax.fori_loop(0, dz, zf, zl, unroll=True)
    y = coef(0, 1, start_z + dz) * cz[dz]
    cz[dz + 1] = zr0 + y
    y = coef(0, 1, start_z + dz + 1) * y
    cz[dz + 2] = zr1 + y
    def zb(i, y):
        r = dz - 1 - i
        y = coef(0, 2, start_z + r) * y
        cz[r + 1] = cz[r + 1] + y
        return y
    y = lax.fori_loop(0, dz, zb, zr0, unroll=True)
    cz[0] = zl + coef(0, 2, start_z - 1) * (uz[0] + y)
    for i in range(dz + 3, zp):
        cz[i] = jnp.zeros((dx, dy), F32)
    for i in range(dx // 8):
        ce[HALO - 1 + 8 * i:HALO - 1 + 8 * i + 8] = jnp.swapaxes(cz[:, 8 * i:8 * i + 8, :], 0, 1)

    def xf(i, y):
        y = coef(1, 0, start_x + i) * ce[HALO - 1 + i] + coef(1, 1, start_x + i) * y
        ux[i] = y
        return y
    lax.fori_loop(0, dx, xf, jnp.zeros((zp, dy), F32), unroll=True)
    def xb(i, y):
        r = dx - 1 - i
        y = coef(1, 2, start_x + r) * y
        ux[r] = ux[r] + y
        return y + coef(1, 0, start_x + r) * ce[HALO - 1 + r]
    lax.fori_loop(0, dx, xb, jnp.zeros((zp, dy), F32), unroll=True)

    def pair(low_src, low_dst, high_src, high_dst, sem, low_id, high_id, low_ok, high_ok):
        low = pltpu.make_async_remote_copy(
            src_ref=low_src, dst_ref=low_dst, send_sem=s_send.at[sem], recv_sem=s_recv.at[sem],
            device_id=low_id, device_id_type=MESH)
        high = pltpu.make_async_remote_copy(
            src_ref=high_src, dst_ref=high_dst, send_sem=s_send.at[sem + 1], recv_sem=s_recv.at[sem + 1],
            device_id=high_id, device_id_type=MESH)
        @pl.when(low_ok)
        def _():
            low.start()
        @pl.when(high_ok)
        def _():
            high.start()
        def wait():
            @pl.when(low_ok)
            def _():
                low.wait_send()
                high.wait_recv()
            @pl.when(high_ok)
            def _():
                high.wait_send()
                low.wait_recv()
        return wait

    nch = zp // 8
    rows = ex // nslot
    for i in range(dx + 2 * HALO - 1, ex):
        ce[i] = jnp.zeros((zp, dy), F32)
    waits_x, waits_y = [], []
    for c in range(nch):
        zs = pl.ds(8 * c, 8)
        waits_x.append(pair(
            ux.at[pl.ds(0, HALO), zs], xr.at[:, zs], ux.at[pl.ds(dx - HALO, HALO), zs], xl.at[:, zs],
            6 + 2 * c, (me_x - 1, me_y, me_z), (me_x + 1, me_y, me_z), has_l, has_r))

    def combine(c):
        zs = pl.ds(8 * c, 8)
        def gf(i, y):
            y = coef(1, 1, start_x + i) * y
            ce[HALO - 1 + i, zs] = ux[i, zs] + y
            return y
        lax.fori_loop(0, dx, gf, xl[HALO - 1, zs], unroll=True)
        def gr(i, y):
            y = coef(1, 1, start_x + dx + i) * y
            ce[HALO - 1 + dx + i, zs] = xr[i, zs] + y
            return y
        lax.fori_loop(0, HALO, gr, ce[HALO - 1 + dx - 1, zs], unroll=True)
        def gb(i, y):
            r = dx - 1 - i
            y = coef(1, 2, start_x + r) * y
            ce[HALO - 1 + r, zs] = ce[HALO - 1 + r, zs] + y
            return y
        y = lax.fori_loop(0, dx, gb, xr[0, zs], unroll=True)
        def gl(i, y):
            y = coef(1, 2, start_x - 1 - i) * y
            ce[HALO - 2 - i, zs] = xl[HALO - 1 - i, zs] + y
            return y
        lax.fori_loop(0, HALO - 1, gl, ux[0, zs] + y, unroll=True)

    n8 = rows * 8
    def pack(c):
        res = split3(ce[:, 8 * c:8 * c + 8, :].reshape(ex * 8, dy), ends3[...])
        low, high = None, None
        for k in range(nslot):
            a = res[n8 * k:n8 * k + n8, :dy]
            b = res[n8 * k:n8 * k + n8, dy:]
            if k > 0:
                a = pltpu.roll(a, HALO * k, 1)
                b = pltpu.roll(b, HALO * k, 1)
            low = a if low is None else low + a
            high = b if high is None else high + b
        packl[c] = low.reshape(rows, 8, dy)
        packr[c] = high.reshape(rows, 8, dy)

    lane3 = iota((n8, dy), 1)
    def spread_y(c):
        left = yl[c].reshape(n8, dy)
        right = yr[c].reshape(n8, dy)
        halos = []
        for k in range(nslot):
            a, b = left, right
            if k > 0:
                a = pltpu.roll(a, dy - HALO * k, 1)
            if k != 1:
                b = pltpu.roll(b, (dy + HALO - HALO * k) % dy, 1)
            halos.append(jnp.where(lane3 < HALO, a, jnp.where(lane3 < 2 * HALO, b, 0.0)))
        own = ce[:, 8 * c:8 * c + 8, :].reshape(ex * 8, dy)
        both = jnp.concatenate([own, jnp.concatenate(halos, axis=0)], axis=1)
        count = (ex - rows) * 8
        g0[:, 8 * c:8 * c + 8, :] = split3(both[:count], w0[...]).reshape(ex - rows, 8, 2 * dy)
        g1[:, 8 * c:8 * c + 8, :] = split3(both[n8:], w1[...]).reshape(ex - rows, 8, 2 * dy)

    for c in range(nch):
        waits_x[c]()
        combine(c)
        pack(c)
        waits_y.append(pair(packl.at[c], yr.at[c], packr.at[c], yl.at[c], 6 + 2 * nch + 2 * c,
                            (me_x, me_y - 1, me_z), (me_x, me_y + 1, me_z), has_d, has_u))
        if c > 0:
            waits_y[c - 1]()
            spread_y(c - 1)
    waits_y[nch - 1]()
    spread_y(nch - 1)

    group2 = jnp.concatenate([group, group], axis=1)
    wsum = []
    for bx, gref in ((0, g0), (1, g1)):
        base = [off[0, bx, by] + RANGE + bx * (BRICK - rows) for by in range(nby)]
        def pick(i, c, gref=gref, base=base):
            v = gref[base[0] + i]
            for by in range(1, nby):
                v = jnp.where(group2 == by, gref[base[by] + i], v)
            hs[i] = v
            return c
        lax.fori_loop(0, BRICK + 3, pick, 0)
        def fir(i, total, bx=bx):
            gx_pos = start_x + bx * BRICK + i + ox_v[bx]
            ok_x = jnp.where((gx_pos >= 0) & (gx_pos < nx), 1.0, 0.0)
            h = [hs[i + c] for c in range(4)]
            hv = [v[:, :dy] for v in h]
            hd = [v[:, dy:] for v in h]
            def comb(w, vs):
                return (w[0] * vs[0] + w[1] * vs[1] + w[2] * vs[2] + w[3] * vs[3]) * ok_x
            val, dxx, dyy = comb(tx, hv), comb(sx, hv), comb(tx, hd)
            def zfir(w, v):
                return w[0] * v[0:dz] + w[1] * v[1:dz + 1] + w[2] * v[2:dz + 2] + w[3] * v[3:dz + 3]
            out = zfir(tz, val)
            r = bx * BRICK + i
            wv[r] = out
            px[r] = zfir(tz, dxx)
            py[r] = zfir(tz, dyy)
            pz[r] = zfir(sz, val)
            return total + out
        total = lax.fori_loop(0, BRICK, fir, jnp.zeros((dz, dy), F32))
        wsum.append(jnp.sum(total, axis=0, keepdims=True))

    mean_w = group_sum(row8(wsum)) / half
    sww, sfw = [], []
    for b in range(nbx):
        cw = wv[BRICK * b:BRICK * b + BRICK] - mean_w[b:b + 1][None]
        wv[BRICK * b:BRICK * b + BRICK] = cw
        cf = ft[BRICK * b:BRICK * b + BRICK]
        sww.append(jnp.sum(jnp.sum(cw * cw, axis=0), axis=0, keepdims=True))
        sfw.append(jnp.sum(jnp.sum(cf * cw, axis=0), axis=0, keepdims=True))
    sums = group_sum(row8(sff + sww + sfw))
    stat[0] = row8([mean_f[b:b + 1] for b in range(nbx)] + [mean_w[b:b + 1] for b in range(nbx)])
    stat[1] = sums
    st_copy = pltpu.make_async_remote_copy(
        src_ref=stat, dst_ref=statr, send_sem=s_send.at[5], recv_sem=s_recv.at[5],
        device_id=(me_x, me_y, other_z), device_id_type=MESH)
    st_copy.start()

    ne = nbx + 4
    xrow = [[0.0] * dx for _ in range(ne)]
    for e in range(ne):
        for r in range(dx):
            u = abs(r - BRICK * (e - 2) - BRICK // 2) / BRICK
            xrow[e][r] = (2.0 / 3.0 - u * u + u ** 3 / 2.0) if u < 1 else max(2.0 - u, 0.0) ** 3 / 6.0
    for d, pref in enumerate((px, py, pz)):
        for b in range(nbx):
            for kind, other in enumerate((ft, wv, None)):
                accs = [None] * 5
                for r in range(BRICK * b, BRICK * b + BRICK):
                    force = pref[r] if other is None else pref[r] * other[r]
                    for e in range(5):
                        if xrow[b + e][r] != 0.0:
                            t = xrow[b + e][r] * force
                            accs[e] = t if accs[e] is None else accs[e] + t
                for e in range(5):
                    proj[((d * nbx + b) * 3 + kind) * 5 + e] = accs[e]
    st_copy.wait()
    voxels = 2.0 * half
    alphas, betas, gammas, nccs = [], [], [], []
    own_m, oth_m = stat[0], statr[0]
    own_s, oth_s = stat[1], statr[1]
    diff = own_m - oth_m
    for b in range(nbx):
        df, dw = diff[b:b + 1], diff[nbx + b:nbx + b + 1]
        def both_halves(i, extra):
            return own_s[i:i + 1] + oth_s[i:i + 1] + extra * (half / 2.0)
        ff = both_halves(b, df * df)
        ww = both_halves(nbx + b, dw * dw)
        fw = both_halves(2 * nbx + b, df * dw)
        inv = lax.rsqrt(ff * ww + EPSILON)
        ratio = fw / (ww + EPSILON)
        nccs.append(fw * inv)
        alphas.append(voxels * inv)
        betas.append(ratio)
        gammas.append(0.5 * (df - ratio * dw))
    every = jnp.where(iota((dy, dy), 0) == BRICK * iota((dy, dy), 1), 1.0, 0.0)
    ncc_rows = jnp.dot(row8(nccs), every, precision=HIGHEST, preferred_element_type=F32)
    ncc_out[...] = ncc_rows[:nbx, :nby]

    zrow = (start_z + iota((dz, 1), 0)).astype(F32)
    bz = [bspline((zrow - float(BRICK * k + BRICK // 2)) / BRICK) for k in range(nz // BRICK)]
    nk = nz // BRICK
    ycol = iota((dy, dy), 1)
    yoff = (iota((dy, dy), 0) - BRICK * (ycol - 2) - BRICK // 2).astype(F32) / BRICK
    by_mat = jnp.where(ycol < nby + 4, bspline(yoff), 0.0)
    for d in range(3):
        accs = [None] * ne
        for b in range(nbx):
            for e in range(5):
                at3 = ((d * nbx + b) * 3) * 5 + e
                t = alphas[b] * (proj[at3] - betas[b] * proj[at3 + 5] + gammas[b] * proj[at3 + 10])
                accs[b + e] = t if accs[b + e] is None else accs[b + e] + t
        for e in range(ne):
            for k in range(nk):
                part[e, d * nk + k:d * nk + k + 1, :] = jnp.sum(accs[e] * bz[k], axis=0, keepdims=True)
    for e in range(ne):
        part[e, 3 * nk:] = jnp.zeros((part.shape[1] - 3 * nk, dy), F32)
    depth = part.shape[1]
    full = jnp.dot(part[...].reshape(ne * depth, dy), by_mat, precision=HIGHEST,
                   preferred_element_type=F32) * (1.0 / SUPPORT_NORM)
    part[...] = full.reshape(ne, depth, dy)

    def slot_of(ix, iy, iz):
        return ((ix + 1) * 3 + (iy + 1)) * 2 + iz

    for ix, iy, iz, ok, target in peers:
        there = slot_of(-ix, -iy, iz)
        here = slot_of(ix, iy, iz)
        @pl.when(jnp.logical_not(ok))
        def _(here=here):
            gather[here] = jnp.zeros(gather.shape[1:], F32)
        @pl.when(ok)
        def _(ix=ix, there=there, target=target):
            pltpu.make_async_remote_copy(
                src_ref=part.at[pl.ds(2 + nbx * ix if ix >= 0 else 0, nbx)],
                dst_ref=gather.at[there], send_sem=f_send.at[there], recv_sem=f_recv.at[there],
                device_id=target, device_id_type=MESH).start()
    for ix, iy, iz, ok, target in peers:
        there = slot_of(-ix, -iy, iz)
        here = slot_of(ix, iy, iz)
        @pl.when(ok)
        def _(ix=ix, there=there, here=here, target=target):
            pltpu.make_async_remote_copy(
                src_ref=part.at[pl.ds(2 + nbx * ix if ix >= 0 else 0, nbx)],
                dst_ref=gather.at[there], send_sem=f_send.at[there], recv_sem=f_recv.at[there],
                device_id=target, device_id_type=MESH).wait_send()
            pltpu.make_async_remote_copy(
                src_ref=part.at[pl.ds(0, nbx)],
                dst_ref=gather.at[here], send_sem=f_send.at[here], recv_sem=f_recv.at[here],
                device_id=target, device_id_type=MESH).wait_recv()
    gather_own = part[2:2 + nbx]
    lane_c = iota((nbx * depth, dy), 1)
    result = None
    for iy in (-1, 0, 1):
        total = gather_own if iy == 0 else None
        for ix in (-1, 0, 1):
            for iz in (0, 1):
                if (ix, iy, iz) == (0, 0, 0):
                    continue
                v = gather[slot_of(ix, iy, iz)]
                total = v if total is None else total + v
        total = total.reshape(nbx * depth, dy)
        if iy == 0:
            moved = pltpu.roll(total, dy - 2, 1)
        elif iy < 0:
            moved = jnp.where(lane_c < 2, pltpu.roll(total, dy - (nby + 2), 1), 0.0)
        else:
            moved = jnp.where(lane_c >= nby - 2, pltpu.roll(total, nby - 2, 1), 0.0)
        result = moved if result is None else result + moved
    for i in range(nbx):
        for d in range(3):
            for k in range(nk):
                row = i * depth + d * nk + k
                grad_out[d, k, i:i + 1, :] = result[row:row + 1, :nby]


def shards(sizes, moving_image, fixed_image, subvoxel, brick_offset):
    nx_dev, ny_dev, nz_dev = sizes
    dz, dx, dy = moving_image.shape
    nz, nx, ny = dz * nz_dev, dx * nx_dev, dy * ny_dev
    table, width_t = factor_tables((nz, nx, ny))
    zp = -(-(dz + 3) // 8) * 8
    nslot = dy // HALO
    ex = -(-(dx + 2 * HALO - 1) // nslot) * nslot
    rows = ex // nslot
    nch = zp // 8
    nbx, nby, nk = dx // BRICK, dy // BRICK, nz // BRICK
    depth = -(-3 * nk // 8) * 8
    cfg = (nx_dev, ny_dev, width_t, nz, nx, ny, dz, dx, dy, zp, ex)
    vm = lambda *shape: pltpu.VMEM(shape, F32)
    vspec = pl.BlockSpec(memory_space=pltpu.VMEM)
    hspec = pl.BlockSpec(memory_space=pl.ANY)
    sspec = pl.BlockSpec(memory_space=pltpu.SMEM)
    return pl.pallas_call(
        functools.partial(kernel, cfg),
        out_shape=(
            jax.ShapeDtypeStruct((nbx, nby), F32),
            jax.ShapeDtypeStruct((3, nk, nbx, nby), F32),
        ),
        in_specs=[sspec, sspec, sspec, hspec, hspec],
        out_specs=(vspec, vspec),
        scratch_shapes=[
            vm(dz, dx, dy), vm(dz, dx, dy), pltpu.SemaphoreType.DMA((2,)),
            vm(dz, dx, dy), vm(2, dx, dy), vm(zp, dx, dy),
            vm(dx, zp, dy), vm(HALO, zp, dy), vm(HALO, zp, dy), vm(ex, zp, dy),
            vm(nch, rows, 8, dy), vm(nch, rows, 8, dy), vm(nch, rows, 8, dy), vm(nch, rows, 8, dy),
            pltpu.VMEM((3 * dy, 2 * dy), BF16),
            pltpu.VMEM((6 * dy, 2 * dy), BF16), pltpu.VMEM((6 * dy, 2 * dy), BF16),
            vm(ex - rows, zp, 2 * dy), vm(ex - rows, zp, 2 * dy), vm(BRICK + 3, zp, 2 * dy),
            vm(dx, dz, dy), vm(dx, dz, dy), vm(dx, dz, dy), vm(dx, dz, dy), vm(dx, dz, dy),
            vm(3 * nbx * 3 * 5, dz, dy),
            vm(2, 8, dy), vm(2, 8, dy),
            vm(nbx + 4, depth, dy), vm(18, nbx, depth, dy),
            pltpu.SemaphoreType.DMA((6 + 4 * nch,)), pltpu.SemaphoreType.DMA((6 + 4 * nch,)),
            pltpu.SemaphoreType.DMA((18,)), pltpu.SemaphoreType.DMA((18,)),
        ],
        compiler_params=pltpu.CompilerParams(
            collective_id=0, has_side_effects=True, vmem_limit_bytes=56 * 1024 * 1024),
    )(jnp.asarray(table), subvoxel, brick_offset, moving_image, fixed_image)


def solution(mesh):
    sizes = (mesh.shape["gx"], mesh.shape["gy"], mesh.shape["gz"])
    return jax.shard_map(
        functools.partial(shards, sizes),
        mesh=mesh,
        in_specs=(P("gz", "gx", "gy"), P("gz", "gx", "gy"), P(), P(None, "gx", "gy")),
        out_specs=(P("gx", "gy"), P(None, None, "gx", "gy")),
        check_vma=False,
    )
```

```python
import functools
import math

import jax
import jax.numpy as jnp
import numpy as np
from jax import lax
from jax.experimental import pallas as pl
from jax.experimental.pallas import tpu as pltpu
from jax.sharding import PartitionSpec as P

BRICK = 16
RANGE = 16
EPSILON = 1e-06
SUPPORT_NORM = 64.0
LOG_POLE = math.log(2.0 + math.sqrt(3.0))
POLE = 2.0 - math.sqrt(3.0)
PAD = 32
HALO = RANGE + 2
F32 = jnp.float32
BF16 = jnp.bfloat16
MESH = pl.DeviceIdType.MESH
HIGHEST = lax.Precision.HIGHEST


def factor_table(length):
    t = np.arange(-PAD, length + PAD, dtype=np.float64) + 1.0
    inside = (t >= 1) & (t <= length)
    ti = np.clip(t, 1, length)
    scale = (1.0 / POLE - POLE) * (1.0 - POLE ** (2.0 * (length + 1)))
    low = 1.0 - POLE ** (2.0 * ti)
    high = 1.0 - POLE ** (2.0 * (length + 1 - ti))
    diag = 6.0 * low * high / scale
    fwd = -POLE * high / (1.0 - POLE ** (2.0 * (length + 2 - ti)))
    bwd = -POLE * low / (1.0 - POLE ** (2.0 * (ti + 1)))
    return [np.where(inside, v, 0.0) for v in (diag, fwd, bwd)]


def factor_tables(lengths):
    width = max(lengths) + 2 * PAD
    rows = []
    for length in lengths:
        for row in factor_table(length):
            rows.append(np.pad(row, (0, width - row.shape[0])))
    return np.stack(rows).astype(np.float32).reshape(-1), width


def inverse_entry(row, col, length):
    nearer = jnp.minimum(row, col).astype(F32) + 1.0
    farther = jnp.maximum(row, col).astype(F32) + 1.0
    entry = jnp.exp((nearer - farther) * LOG_POLE) * (1.0 - jnp.exp(-2.0 * LOG_POLE * nearer))
    entry = entry * (1.0 - jnp.exp(-2.0 * LOG_POLE * (length + 1 - farther)))
    entry = entry * (
        6.0 / ((1.0 / POLE - POLE) * (1.0 - math.exp(-2.0 * LOG_POLE * (length + 1))))
    )
    parity = 1.0 - 2.0 * ((row + col) & 1).astype(F32)
    return entry * parity


def iota(shape, dim):
    return lax.broadcasted_iota(jnp.int32, shape, dim)


def split3(left, right):
    left_hi = left.astype(BF16)
    left_lo = (left - left_hi.astype(F32)).astype(BF16)
    lhs = jnp.concatenate([left_hi, left_hi, left_lo], axis=1)
    return jnp.dot(lhs, right, preferred_element_type=F32)


def stack3(right):
    right_hi = right.astype(BF16)
    right_lo = (right - right_hi.astype(F32)).astype(BF16)
    return jnp.concatenate([right_hi, right_lo, right_hi], axis=0)


def bspline(offset):
    magnitude = jnp.abs(offset)
    inner = 2.0 / 3.0 - magnitude * magnitude + 0.5 * magnitude * magnitude * magnitude
    rest = jnp.maximum(2.0 - magnitude, 0.0)
    outer = rest * rest * rest / 6.0
    return jnp.where(magnitude < 1.0, inner, outer)


def taps_of(t):
    smooth = (
        (1.0 - t) * (1.0 - t) * (1.0 - t) / 6.0,
        (3.0 * t * t * t - 6.0 * t * t + 4.0) / 6.0,
        (-3.0 * t * t * t + 3.0 * t * t + 3.0 * t + 1.0) / 6.0,
        t * t * t / 6.0,
    )
    slope = (
        -((1.0 - t) * (1.0 - t)) / 2.0,
        (3.0 * t * t - 4.0 * t) / 2.0,
        (-3.0 * t * t + 2.0 * t + 1.0) / 2.0,
        t * t / 2.0,
    )
    return smooth, slope


def kernel(
    cfg, table, sub, off, img_hbm, fix_hbm, ncc_out, grad_out,
    img, fix, in_sem, uz, zrecv, cz, ux, xl, xr, ce, packl, packr, yl, yr, ends3, w0, w1, g0, g1, hs,
    ft, wv, px, py, pz, proj, stat, statr, part, out_tiles, gather,
    s_send, s_recv, f_send, f_recv,
):
    (nx_dev, ny_dev, width_t, nz, nx, ny, dz, dx, dy, zp, ex) = cfg
    zu = -(-(dz + 3) // 4) * 4
    me_x, me_y, me_z = (lax.axis_index(a) for a in ("gx", "gy", "gz"))
    other_z = 1 - me_z
    start_x, start_y, start_z = me_x * dx, me_y * dy, me_z * dz
    nbx, nby = dx // BRICK, dy // BRICK

    load_img = pltpu.make_async_copy(img_hbm, img, in_sem.at[0])
    load_fix = pltpu.make_async_copy(fix_hbm, fix, in_sem.at[1])
    load_img.start()
    load_fix.start()

    peers = []
    for ix in (-1, 0, 1):
        for iy in (-1, 0, 1):
            for iz in (0, 1):
                if (ix, iy, iz) == (0, 0, 0):
                    continue
                px_, py_ = me_x + ix, me_y + iy
                ok = (px_ >= 0) & (px_ < nx_dev) & (py_ >= 0) & (py_ < ny_dev)
                target = (px_, py_, other_z if iz else me_z)
                peers.append((ix, iy, iz, ok, target))
    barrier = pltpu.get_barrier_semaphore()
    count = jnp.int32(0)
    for ix, iy, iz, ok, target in peers:
        if abs(ix) + abs(iy) + iz > 1:
            continue
        @pl.when(ok)
        def _(target=target):
            pl.semaphore_signal(barrier, inc=1, device_id=target, device_id_type=MESH)
        count = count + ok.astype(jnp.int32)

    def coef(axis, kind, pos):
        return table[(3 * axis + kind) * width_t + PAD + pos]

    load_img.wait()
    def zbody(i, state):
        state = coef(0, 0, start_z + i) * img[i] + coef(0, 1, start_z + i) * state
        uz[i] = state
        return state
    lax.fori_loop(0, dz, zbody, jnp.zeros((dx, dy), F32), unroll=True)
    def zback(i, state):
        r = dz - 1 - i
        state = coef(0, 2, start_z + r) * state
        uz[r] = uz[r] + state
        return state + coef(0, 0, start_z + r) * img[r]
    lax.fori_loop(0, dz, zback, jnp.zeros((dx, dy), F32), unroll=True)

    has_l, has_r = me_x > 0, me_x < nx_dev - 1
    has_d, has_u = me_y > 0, me_y < ny_dev - 1
    for have, ref in ((has_l, xl), (has_r, xr), (has_d, yl), (has_u, yr)):
        @pl.when(jnp.logical_not(have))
        def _(ref=ref):
            ref[...] = jnp.zeros(ref.shape, F32)

    if zu < zp:
        xl[:, zu:] = jnp.zeros((HALO, zp - zu, dy), F32)
        xr[:, zu:] = jnp.zeros((HALO, zp - zu, dy), F32)

    tz, sz = taps_of(sub[0])
    tx, sx = taps_of(sub[1])
    ty, sy = taps_of(sub[2])
    lane = iota((1, dy), 1)
    group = lane // BRICK
    ox_v, oy_v = [], []
    for bx in range(nbx):
        vx = jnp.zeros((1, dy), jnp.int32)
        vy = jnp.zeros((1, dy), jnp.int32)
        for by in range(nby):
            vx = jnp.where(group == by, off[0, bx, by], vx)
            vy = jnp.where(group == by, off[1, bx, by], vy)
        ox_v.append(vx)
        oy_v.append(vy)

    nslot = dy // HALO
    col = iota((dy, 2 * dy), 1)
    src = iota((dy, 2 * dy), 0)
    lane_in = jnp.where(col < dy, col, col - dy)
    slot = lane_in // HALO
    at = lane_in - slot * HALO + jnp.where(col < dy, 0, dy - HALO)
    ends3[...] = stack3(jnp.where(slot == 0, inverse_entry(start_y + at, start_y + src, ny), 0.0))

    wide = 2 * dy
    jcol = iota((dy, wide), 1) - HALO
    jin = (start_y + jcol >= 0) & (start_y + jcol < ny) & (jcol < dy + HALO)
    own_part = jnp.where(jin, inverse_entry(
        jnp.clip(start_y + jcol, 0, ny - 1), start_y + iota((dy, wide), 0), ny), 0.0)
    m = iota((dy, wide), 0)
    jf = (start_y + jcol + 1).astype(F32)
    parity = 1.0 - 2.0 * (jcol & 1).astype(F32)
    t_left = (start_y * jnp.ones((1, 1), jnp.int32)).astype(F32)
    t_right = t_left + float(dy + 1)
    high = 1.0 - jnp.exp(-2.0 * LOG_POLE * (ny + 1 - jf))
    low = 1.0 - jnp.exp(-2.0 * LOG_POLE * jf)
    jown = jcol.astype(F32)
    from_left = -parity * jnp.exp(-LOG_POLE * (jown + 1.0)) * high / (
        1.0 - jnp.exp(-2.0 * LOG_POLE * (ny + 1 - t_left)))
    from_right = parity * jnp.exp(LOG_POLE * (jown - float(dy))) * low / (
        1.0 - jnp.exp(-2.0 * LOG_POLE * t_right))
    if dy % 2:
        from_right = -from_right
    left_col = jnp.where(jcol < 0, jnp.where(m - HALO == jcol, 1.0, 0.0),
                         jnp.where(m == HALO - 1, from_left, 0.0))
    right_col = jnp.where(jcol >= dy, jnp.where(m - HALO + dy == jcol, 1.0, 0.0),
                          jnp.where(m == HALO, from_right, 0.0))
    halo_part = jnp.where(m < HALO, left_col, jnp.where(m < 2 * HALO, right_col, 0.0))
    halo_part = jnp.where(jin, halo_part, 0.0)
    full_y = jnp.concatenate([own_part, halo_part], axis=0)
    for bx, wref in ((0, w0), (1, w1)):
        jrow = iota((wide, dy), 0) - HALO
        want = lane + oy_v[bx]
        ok_y = jnp.where((start_y + want >= 0) & (start_y + want < ny), 1.0, 0.0)
        picks = []
        for taps in (ty, sy):
            acc = jnp.zeros((wide, dy), F32)
            for c in range(4):
                acc = jnp.where(jrow == want + (c - 1), taps[c], acc)
            picks.append(acc * ok_y)
        wref[...] = stack3(jnp.dot(full_y, jnp.concatenate(picks, axis=1), precision=HIGHEST,
                                   preferred_element_type=F32))

    ones = jnp.where(iota((dy, dy), 0) // BRICK == iota((dy, dy), 1) // BRICK, 1.0, 0.0)
    half = float(dz * BRICK * BRICK)

    def group_sum(rows):
        return jnp.dot(rows, ones, precision=HIGHEST, preferred_element_type=F32)

    def row8(vecs):
        rows = iota((8, dy), 0)
        out = jnp.zeros((8, dy), F32)
        for i, v in enumerate(vecs):
            out = jnp.where(rows == i, v, out)
        return out

    load_fix.wait()
    for i in range(dx // 8):
        ft[8 * i:8 * i + 8] = jnp.swapaxes(fix[:, 8 * i:8 * i + 8, :], 0, 1)
    fsum = [jnp.sum(jnp.sum(ft[BRICK * b:BRICK * b + BRICK], axis=0), axis=0, keepdims=True) for b in range(nbx)]
    mean_f = group_sum(row8(fsum)) / half
    sff = []
    for b in range(nbx):
        cf = ft[BRICK * b:BRICK * b + BRICK] - mean_f[b:b + 1][None]
        ft[BRICK * b:BRICK * b + BRICK] = cf
        sff.append(jnp.sum(jnp.sum(cf * cf, axis=0), axis=0, keepdims=True))

    pl.semaphore_wait(barrier, count)
    first = jnp.where(me_z == 0, dz - 2, 0)
    z_copy = pltpu.make_async_remote_copy(
        src_ref=uz.at[pl.ds(first, 2)], dst_ref=zrecv, send_sem=s_send.at[0], recv_sem=s_recv.at[0],
        device_id=(me_x, me_y, other_z), device_id_type=MESH)
    z_copy.start()

    z_copy.wait()
    left_on = jnp.where(me_z == 1, 1.0, 0.0)
    right_on = 1.0 - left_on
    zl = zrecv[1] * left_on
    zr0, zr1 = zrecv[0] * right_on, zrecv[1] * right_on
    def zf(i, y):
        y = coef(0, 1, start_z + i) * y
        cz[i + 1] = uz[i] + y
        return y
    lax.fori_loop(0, dz, zf, zl, unroll=True)
    y = coef(0, 1, start_z + dz) * cz[dz]
    cz[dz + 1] = zr0 + y
    y = coef(0, 1, start_z + dz + 1) * y
    cz[dz + 2] = zr1 + y
    def zb(i, y):
        r = dz - 1 - i
        y = coef(0, 2, start_z + r) * y
        cz[r + 1] = cz[r + 1] + y
        return y
    y = lax.fori_loop(0, dz, zb, zr0, unroll=True)
    cz[0] = zl + coef(0, 2, start_z - 1) * (uz[0] + y)
    for i in range(dz + 3, zp):
        cz[i] = jnp.zeros((dx, dy), F32)
    for i in range(dx // 8):
        ce[HALO - 1 + 8 * i:HALO - 1 + 8 * i + 8] = jnp.swapaxes(cz[:, 8 * i:8 * i + 8, :], 0, 1)

    def xf(i, y):
        y = coef(1, 0, start_x + i) * ce[HALO - 1 + i] + coef(1, 1, start_x + i) * y
        ux[i] = y
        return y
    lax.fori_loop(0, dx, xf, jnp.zeros((zp, dy), F32), unroll=True)
    def xb(i, y):
        r = dx - 1 - i
        y = coef(1, 2, start_x + r) * y
        ux[r] = ux[r] + y
        return y + coef(1, 0, start_x + r) * ce[HALO - 1 + r]
    lax.fori_loop(0, dx, xb, jnp.zeros((zp, dy), F32), unroll=True)

    def pair(low_src, low_dst, high_src, high_dst, sem, low_id, high_id, low_ok, high_ok):
        low = pltpu.make_async_remote_copy(
            src_ref=low_src, dst_ref=low_dst, send_sem=s_send.at[sem], recv_sem=s_recv.at[sem],
            device_id=low_id, device_id_type=MESH)
        high = pltpu.make_async_remote_copy(
            src_ref=high_src, dst_ref=high_dst, send_sem=s_send.at[sem + 1], recv_sem=s_recv.at[sem + 1],
            device_id=high_id, device_id_type=MESH)
        @pl.when(low_ok)
        def _():
            low.start()
        @pl.when(high_ok)
        def _():
            high.start()
        def wait():
            @pl.when(low_ok)
            def _():
                low.wait_send()
                high.wait_recv()
            @pl.when(high_ok)
            def _():
                high.wait_send()
                low.wait_recv()
        return wait

    nch = zp // 8
    rows = ex // nslot
    for i in range(dx + 2 * HALO - 1, ex):
        ce[i] = jnp.zeros((zp, dy), F32)
    waits_x, waits_y = [], []
    for c in range(nch):
        zs = pl.ds(8 * c, min(8, zu - 8 * c))
        waits_x.append(pair(
            ux.at[pl.ds(0, HALO), zs], xr.at[:, zs], ux.at[pl.ds(dx - HALO, HALO), zs], xl.at[:, zs],
            6 + 2 * c, (me_x - 1, me_y, me_z), (me_x + 1, me_y, me_z), has_l, has_r))

    def combine(c):
        zs = pl.ds(8 * c, 8)
        def gf(i, y):
            y = coef(1, 1, start_x + i) * y
            ce[HALO - 1 + i, zs] = ux[i, zs] + y
            return y
        lax.fori_loop(0, dx, gf, xl[HALO - 1, zs], unroll=True)
        def gr(i, y):
            y = coef(1, 1, start_x + dx + i) * y
            ce[HALO - 1 + dx + i, zs] = xr[i, zs] + y
            return y
        lax.fori_loop(0, HALO, gr, ce[HALO - 1 + dx - 1, zs], unroll=True)
        def gb(i, y):
            r = dx - 1 - i
            y = coef(1, 2, start_x + r) * y
            ce[HALO - 1 + r, zs] = ce[HALO - 1 + r, zs] + y
            return y
        y = lax.fori_loop(0, dx, gb, xr[0, zs], unroll=True)
        def gl(i, y):
            y = coef(1, 2, start_x - 1 - i) * y
            ce[HALO - 2 - i, zs] = xl[HALO - 1 - i, zs] + y
            return y
        lax.fori_loop(0, HALO - 1, gl, ux[0, zs] + y, unroll=True)

    n8 = rows * 8
    def pack(c):
        res = split3(ce[:, 8 * c:8 * c + 8, :].reshape(ex * 8, dy), ends3[...])
        low, high = None, None
        for k in range(nslot):
            a = res[n8 * k:n8 * k + n8, :dy]
            b = res[n8 * k:n8 * k + n8, dy:]
            if k > 0:
                a = pltpu.roll(a, HALO * k, 1)
                b = pltpu.roll(b, HALO * k, 1)
            low = a if low is None else low + a
            high = b if high is None else high + b
        packl[c] = low.reshape(rows, 8, dy)
        packr[c] = high.reshape(rows, 8, dy)

    lane3 = iota((n8, dy), 1)
    def spread_y(c):
        left = yl[c].reshape(n8, dy)
        right = yr[c].reshape(n8, dy)
        halos = []
        for k in range(nslot):
            a, b = left, right
            if k > 0:
                a = pltpu.roll(a, dy - HALO * k, 1)
            if k != 1:
                b = pltpu.roll(b, (dy + HALO - HALO * k) % dy, 1)
            halos.append(jnp.where(lane3 < HALO, a, jnp.where(lane3 < 2 * HALO, b, 0.0)))
        own = ce[:, 8 * c:8 * c + 8, :].reshape(ex * 8, dy)
        both = jnp.concatenate([own, jnp.concatenate(halos, axis=0)], axis=1)
        count = (ex - rows) * 8
        g0[:, 8 * c:8 * c + 8, :] = split3(both[:count], w0[...]).reshape(ex - rows, 8, 2 * dy)
        g1[:, 8 * c:8 * c + 8, :] = split3(both[n8:], w1[...]).reshape(ex - rows, 8, 2 * dy)

    for c in range(nch):
        waits_x[c]()
        combine(c)
        pack(c)
        waits_y.append(pair(packl.at[c], yr.at[c], packr.at[c], yl.at[c], 6 + 2 * nch + 2 * c,
                            (me_x, me_y - 1, me_z), (me_x, me_y + 1, me_z), has_d, has_u))
        if c > 0:
            waits_y[c - 1]()
            spread_y(c - 1)
    waits_y[nch - 1]()
    spread_y(nch - 1)

    group2 = jnp.concatenate([group, group], axis=1)
    wsum = []
    for bx, gref in ((0, g0), (1, g1)):
        base = [off[0, bx, by] + RANGE + bx * (BRICK - rows) for by in range(nby)]
        def pick(i, c, gref=gref, base=base):
            v = gref[base[0] + i]
            for by in range(1, nby):
                v = jnp.where(group2 == by, gref[base[by] + i], v)
            hs[i] = v
            return c
        lax.fori_loop(0, BRICK + 3, pick, 0)
        def fir(i, total, bx=bx):
            gx_pos = start_x + bx * BRICK + i + ox_v[bx]
            ok_x = jnp.where((gx_pos >= 0) & (gx_pos < nx), 1.0, 0.0)
            h = [hs[i + c] for c in range(4)]
            hv = [v[:, :dy] for v in h]
            hd = [v[:, dy:] for v in h]
            def comb(w, vs):
                return (w[0] * vs[0] + w[1] * vs[1] + w[2] * vs[2] + w[3] * vs[3]) * ok_x
            val, dxx, dyy = comb(tx, hv), comb(sx, hv), comb(tx, hd)
            def zfir(w, v):
                return w[0] * v[0:dz] + w[1] * v[1:dz + 1] + w[2] * v[2:dz + 2] + w[3] * v[3:dz + 3]
            out = zfir(tz, val)
            r = bx * BRICK + i
            wv[r] = out
            px[r] = zfir(tz, dxx)
            py[r] = zfir(tz, dyy)
            pz[r] = zfir(sz, val)
            return total + out
        total = lax.fori_loop(0, BRICK, fir, jnp.zeros((dz, dy), F32))
        wsum.append(jnp.sum(total, axis=0, keepdims=True))

    mean_w = group_sum(row8(wsum)) / half
    sww, sfw = [], []
    for b in range(nbx):
        cw = wv[BRICK * b:BRICK * b + BRICK] - mean_w[b:b + 1][None]
        wv[BRICK * b:BRICK * b + BRICK] = cw
        cf = ft[BRICK * b:BRICK * b + BRICK]
        sww.append(jnp.sum(jnp.sum(cw * cw, axis=0), axis=0, keepdims=True))
        sfw.append(jnp.sum(jnp.sum(cf * cw, axis=0), axis=0, keepdims=True))
    sums = group_sum(row8(sff + sww + sfw))
    stat[0] = row8([mean_f[b:b + 1] for b in range(nbx)] + [mean_w[b:b + 1] for b in range(nbx)])
    stat[1] = sums
    st_copy = pltpu.make_async_remote_copy(
        src_ref=stat, dst_ref=statr, send_sem=s_send.at[5], recv_sem=s_recv.at[5],
        device_id=(me_x, me_y, other_z), device_id_type=MESH)
    st_copy.start()

    ne = nbx + 4
    xrow = [[0.0] * dx for _ in range(ne)]
    for e in range(ne):
        for r in range(dx):
            u = abs(r - BRICK * (e - 2) - BRICK // 2) / BRICK
            xrow[e][r] = (2.0 / 3.0 - u * u + u ** 3 / 2.0) if u < 1 else max(2.0 - u, 0.0) ** 3 / 6.0
    for d, pref in enumerate((px, py, pz)):
        for b in range(nbx):
            for kind, other in enumerate((ft, wv, None)):
                accs = [None] * 5
                for r in range(BRICK * b, BRICK * b + BRICK):
                    force = pref[r] if other is None else pref[r] * other[r]
                    for e in range(5):
                        if xrow[b + e][r] != 0.0:
                            t = xrow[b + e][r] * force
                            accs[e] = t if accs[e] is None else accs[e] + t
                for e in range(5):
                    proj[((d * nbx + b) * 3 + kind) * 5 + e] = accs[e]
    st_copy.wait()
    voxels = 2.0 * half
    alphas, betas, gammas, nccs = [], [], [], []
    own_m, oth_m = stat[0], statr[0]
    own_s, oth_s = stat[1], statr[1]
    diff = own_m - oth_m
    for b in range(nbx):
        df, dw = diff[b:b + 1], diff[nbx + b:nbx + b + 1]
        def both_halves(i, extra):
            return own_s[i:i + 1] + oth_s[i:i + 1] + extra * (half / 2.0)
        ff = both_halves(b, df * df)
        ww = both_halves(nbx + b, dw * dw)
        fw = both_halves(2 * nbx + b, df * dw)
        inv = lax.rsqrt(ff * ww + EPSILON)
        ratio = fw / (ww + EPSILON)
        nccs.append(fw * inv)
        alphas.append(voxels * inv)
        betas.append(ratio)
        gammas.append(0.5 * (df - ratio * dw))
    every = jnp.where(iota((dy, dy), 0) == BRICK * iota((dy, dy), 1), 1.0, 0.0)
    ncc_rows = jnp.dot(row8(nccs), every, precision=HIGHEST, preferred_element_type=F32)
    ncc_out[...] = ncc_rows[:nbx, :nby]

    zrow = (start_z + iota((dz, 1), 0)).astype(F32)
    bz = [bspline((zrow - float(BRICK * k + BRICK // 2)) / BRICK) for k in range(nz // BRICK)]
    nk = nz // BRICK
    ycol = iota((dy, dy), 1)
    yoff = (iota((dy, dy), 0) - BRICK * (ycol - 2) - BRICK // 2).astype(F32) / BRICK
    by_mat = jnp.where(ycol < nby + 4, bspline(yoff), 0.0)
    for d in range(3):
        accs = [None] * ne
        for b in range(nbx):
            for e in range(5):
                at3 = ((d * nbx + b) * 3) * 5 + e
                t = alphas[b] * (proj[at3] - betas[b] * proj[at3 + 5] + gammas[b] * proj[at3 + 10])
                accs[b + e] = t if accs[b + e] is None else accs[b + e] + t
        for e in range(ne):
            for k in range(nk):
                row = e * 3 * nk + d * nk + k
                part[row:row + 1, :] = jnp.sum(accs[e] * bz[k], axis=0, keepdims=True)
    full = jnp.dot(part[...], by_mat, precision=HIGHEST, preferred_element_type=F32) * (1.0 / SUPPORT_NORM)
    tiles = nbx * 3 * nk // 8
    for ix in range(3):
        first_row = (0, 2, nbx + 2)[ix] * 3 * nk
        tile = None
        for g in range(tiles):
            t = full[first_row + 8 * g:first_row + 8 * g + 8]
            t = t if g == 0 else pltpu.roll(t, 16 * g, 1)
            tile = t if tile is None else tile + t
        out_tiles[ix] = tile

    def slot_of(ix, iy, iz):
        return ((ix + 1) * 3 + (iy + 1)) * 2 + iz

    for ix, iy, iz, ok, target in peers:
        there = slot_of(-ix, -iy, iz)
        here = slot_of(ix, iy, iz)
        @pl.when(jnp.logical_not(ok))
        def _(here=here):
            gather[here] = jnp.zeros(gather.shape[1:], F32)
        @pl.when(ok)
        def _(ix=ix, there=there, target=target):
            pltpu.make_async_remote_copy(
                src_ref=out_tiles.at[ix + 1],
                dst_ref=gather.at[there], send_sem=f_send.at[there], recv_sem=f_recv.at[there],
                device_id=target, device_id_type=MESH).start()
    for ix, iy, iz, ok, target in peers:
        there = slot_of(-ix, -iy, iz)
        here = slot_of(ix, iy, iz)
        @pl.when(ok)
        def _(ix=ix, there=there, here=here, target=target):
            pltpu.make_async_remote_copy(
                src_ref=out_tiles.at[ix + 1],
                dst_ref=gather.at[there], send_sem=f_send.at[there], recv_sem=f_recv.at[there],
                device_id=target, device_id_type=MESH).wait_send()
            pltpu.make_async_remote_copy(
                src_ref=out_tiles.at[0],
                dst_ref=gather.at[here], send_sem=f_send.at[here], recv_sem=f_recv.at[here],
                device_id=target, device_id_type=MESH).wait_recv()
    gather_own = out_tiles[1]
    lane_c = iota((8, dy), 1) & 15
    result = None
    for iy in (-1, 0, 1):
        total = gather_own if iy == 0 else None
        for ix in (-1, 0, 1):
            for iz in (0, 1):
                if (ix, iy, iz) == (0, 0, 0):
                    continue
                v = gather[slot_of(ix, iy, iz)]
                total = v if total is None else total + v
        if iy == 0:
            moved = pltpu.roll(total, dy - 2, 1)
        elif iy < 0:
            moved = jnp.where(lane_c < 2, pltpu.roll(total, dy - (nby + 2), 1), 0.0)
        else:
            moved = jnp.where(lane_c >= nby - 2, pltpu.roll(total, nby - 2, 1), 0.0)
        result = moved if result is None else result + moved
    for g in range(tiles):
        t = result if g == 0 else pltpu.roll(result, dy - 16 * g, 1)
        for q in range(8):
            i, rest = divmod(8 * g + q, 3 * nk)
            d, k = divmod(rest, nk)
            grad_out[d, k, i:i + 1, :] = t[q:q + 1, :nby]


def shards(sizes, moving_image, fixed_image, subvoxel, brick_offset):
    nx_dev, ny_dev, nz_dev = sizes
    dz, dx, dy = moving_image.shape
    nz, nx, ny = dz * nz_dev, dx * nx_dev, dy * ny_dev
    table, width_t = factor_tables((nz, nx, ny))
    zp = -(-(dz + 3) // 8) * 8
    nslot = dy // HALO
    ex = -(-(dx + 2 * HALO - 1) // nslot) * nslot
    rows = ex // nslot
    nch = zp // 8
    nbx, nby, nk = dx // BRICK, dy // BRICK, nz // BRICK
    cfg = (nx_dev, ny_dev, width_t, nz, nx, ny, dz, dx, dy, zp, ex)
    vm = lambda *shape: pltpu.VMEM(shape, F32)
    vspec = pl.BlockSpec(memory_space=pltpu.VMEM)
    hspec = pl.BlockSpec(memory_space=pl.ANY)
    sspec = pl.BlockSpec(memory_space=pltpu.SMEM)
    return pl.pallas_call(
        functools.partial(kernel, cfg),
        out_shape=(
            jax.ShapeDtypeStruct((nbx, nby), F32),
            jax.ShapeDtypeStruct((3, nk, nbx, nby), F32),
        ),
        in_specs=[sspec, sspec, sspec, hspec, hspec],
        out_specs=(vspec, vspec),
        scratch_shapes=[
            vm(dz, dx, dy), vm(dz, dx, dy), pltpu.SemaphoreType.DMA((2,)),
            vm(dz, dx, dy), vm(2, dx, dy), vm(zp, dx, dy),
            vm(dx, zp, dy), vm(HALO, zp, dy), vm(HALO, zp, dy), vm(ex, zp, dy),
            vm(nch, rows, 8, dy), vm(nch, rows, 8, dy), vm(nch, rows, 8, dy), vm(nch, rows, 8, dy),
            pltpu.VMEM((3 * dy, 2 * dy), BF16),
            pltpu.VMEM((6 * dy, 2 * dy), BF16), pltpu.VMEM((6 * dy, 2 * dy), BF16),
            vm(ex - rows, zp, 2 * dy), vm(ex - rows, zp, 2 * dy), vm(BRICK + 3, zp, 2 * dy),
            vm(dx, dz, dy), vm(dx, dz, dy), vm(dx, dz, dy), vm(dx, dz, dy), vm(dx, dz, dy),
            vm(3 * nbx * 3 * 5, dz, dy),
            vm(2, 8, dy), vm(2, 8, dy),
            vm((nbx + 4) * 3 * nk, dy), vm(3, 8, dy), vm(18, 8, dy),
            pltpu.SemaphoreType.DMA((6 + 4 * nch,)), pltpu.SemaphoreType.DMA((6 + 4 * nch,)),
            pltpu.SemaphoreType.DMA((18,)), pltpu.SemaphoreType.DMA((18,)),
        ],
        compiler_params=pltpu.CompilerParams(
            collective_id=0, has_side_effects=True, vmem_limit_bytes=56 * 1024 * 1024),
    )(jnp.asarray(table), subvoxel, brick_offset, moving_image, fixed_image)


def solution(mesh):
    sizes = (mesh.shape["gx"], mesh.shape["gy"], mesh.shape["gz"])
    return jax.shard_map(
        functools.partial(shards, sizes),
        mesh=mesh,
        in_specs=(P("gz", "gx", "gy"), P("gz", "gx", "gy"), P(), P(None, "gx", "gy")),
        out_specs=(P("gx", "gy"), P(None, None, "gx", "gy")),
        check_vma=False,
    )
```

```python
import functools
import math

import jax
import jax.numpy as jnp
import numpy as np
from jax import lax
from jax.experimental import pallas as pl
from jax.experimental.pallas import tpu as pltpu
from jax.sharding import PartitionSpec as P

BRICK = 16
RANGE = 16
EPSILON = 1e-06
SUPPORT_NORM = 64.0
LOG_POLE = math.log(2.0 + math.sqrt(3.0))
POLE = 2.0 - math.sqrt(3.0)
PAD = 32
HALO = RANGE + 2
F32 = jnp.float32
BF16 = jnp.bfloat16
MESH = pl.DeviceIdType.MESH
HIGHEST = lax.Precision.HIGHEST


def factor_table(length):
    t = np.arange(-PAD, length + PAD, dtype=np.float64) + 1.0
    inside = (t >= 1) & (t <= length)
    ti = np.clip(t, 1, length)
    scale = (1.0 / POLE - POLE) * (1.0 - POLE ** (2.0 * (length + 1)))
    low = 1.0 - POLE ** (2.0 * ti)
    high = 1.0 - POLE ** (2.0 * (length + 1 - ti))
    diag = 6.0 * low * high / scale
    fwd = -POLE * high / (1.0 - POLE ** (2.0 * (length + 2 - ti)))
    bwd = -POLE * low / (1.0 - POLE ** (2.0 * (ti + 1)))
    return [np.where(inside, v, 0.0) for v in (diag, fwd, bwd)]


def factor_tables(lengths):
    width = max(lengths) + 2 * PAD
    rows = []
    for length in lengths:
        for row in factor_table(length):
            rows.append(np.pad(row, (0, width - row.shape[0])))
    return np.stack(rows).astype(np.float32).reshape(-1), width


def inverse_entry(row, col, length):
    nearer = jnp.minimum(row, col).astype(F32) + 1.0
    farther = jnp.maximum(row, col).astype(F32) + 1.0
    entry = jnp.exp((nearer - farther) * LOG_POLE) * (1.0 - jnp.exp(-2.0 * LOG_POLE * nearer))
    entry = entry * (1.0 - jnp.exp(-2.0 * LOG_POLE * (length + 1 - farther)))
    entry = entry * (
        6.0 / ((1.0 / POLE - POLE) * (1.0 - math.exp(-2.0 * LOG_POLE * (length + 1))))
    )
    parity = 1.0 - 2.0 * ((row + col) & 1).astype(F32)
    return entry * parity


def iota(shape, dim):
    return lax.broadcasted_iota(jnp.int32, shape, dim)


def split3(left, right):
    left_hi = left.astype(BF16)
    left_lo = (left - left_hi.astype(F32)).astype(BF16)
    lhs = jnp.concatenate([left_hi, left_hi, left_lo], axis=1)
    return jnp.dot(lhs, right, preferred_element_type=F32)


def stack3(right):
    right_hi = right.astype(BF16)
    right_lo = (right - right_hi.astype(F32)).astype(BF16)
    return jnp.concatenate([right_hi, right_lo, right_hi], axis=0)


def bspline(offset):
    magnitude = jnp.abs(offset)
    inner = 2.0 / 3.0 - magnitude * magnitude + 0.5 * magnitude * magnitude * magnitude
    rest = jnp.maximum(2.0 - magnitude, 0.0)
    outer = rest * rest * rest / 6.0
    return jnp.where(magnitude < 1.0, inner, outer)


def taps_of(t):
    smooth = (
        (1.0 - t) * (1.0 - t) * (1.0 - t) / 6.0,
        (3.0 * t * t * t - 6.0 * t * t + 4.0) / 6.0,
        (-3.0 * t * t * t + 3.0 * t * t + 3.0 * t + 1.0) / 6.0,
        t * t * t / 6.0,
    )
    slope = (
        -((1.0 - t) * (1.0 - t)) / 2.0,
        (3.0 * t * t - 4.0 * t) / 2.0,
        (-3.0 * t * t + 2.0 * t + 1.0) / 2.0,
        t * t / 2.0,
    )
    return smooth, slope


def kernel(
    cfg, table, sub, off, img_hbm, fix_hbm, ncc_out, grad_out,
    img, fix, in_sem, uz, zrecv, cz, ux, xl, xr, ce, packl, packr, yl, yr, ends3, w0, w1, g0, g1, hs,
    ft, wv, px, py, pz, proj, stat, statr, part, out_tiles, gather,
    s_send, s_recv, f_send, f_recv,
):
    (nx_dev, ny_dev, width_t, nz, nx, ny, dz, dx, dy, zp, ex) = cfg
    me_x, me_y, me_z = (lax.axis_index(a) for a in ("gx", "gy", "gz"))
    other_z = 1 - me_z
    start_x, start_y, start_z = me_x * dx, me_y * dy, me_z * dz
    nbx, nby = dx // BRICK, dy // BRICK

    load_img = pltpu.make_async_copy(img_hbm, img, in_sem.at[0])
    load_fix = pltpu.make_async_copy(fix_hbm, fix, in_sem.at[1])
    load_img.start()
    load_fix.start()

    peers = []
    for ix in (-1, 0, 1):
        for iy in (-1, 0, 1):
            for iz in (0, 1):
                if (ix, iy, iz) == (0, 0, 0):
                    continue
                px_, py_ = me_x + ix, me_y + iy
                ok = (px_ >= 0) & (px_ < nx_dev) & (py_ >= 0) & (py_ < ny_dev)
                target = (px_, py_, other_z if iz else me_z)
                peers.append((ix, iy, iz, ok, target))
    barrier = pltpu.get_barrier_semaphore()
    count = jnp.int32(0)
    for ix, iy, iz, ok, target in peers:
        if abs(ix) + abs(iy) + iz > 1:
            continue
        @pl.when(ok)
        def _(target=target):
            pl.semaphore_signal(barrier, inc=1, device_id=target, device_id_type=MESH)
        count = count + ok.astype(jnp.int32)

    def coef(axis, kind, pos):
        return table[(3 * axis + kind) * width_t + PAD + pos]

    load_img.wait()
    def zbody(i, state):
        state = coef(0, 0, start_z + i) * img[i] + coef(0, 1, start_z + i) * state
        uz[i] = state
        return state
    lax.fori_loop(0, dz, zbody, jnp.zeros((dx, dy), F32), unroll=True)
    def zback(i, state):
        r = dz - 1 - i
        state = coef(0, 2, start_z + r) * state
        uz[r] = uz[r] + state
        return state + coef(0, 0, start_z + r) * img[r]
    lax.fori_loop(0, dz, zback, jnp.zeros((dx, dy), F32), unroll=True)

    pl.semaphore_wait(barrier, count)
    first = jnp.where(me_z == 0, dz - 2, 0)
    z_copy = pltpu.make_async_remote_copy(
        src_ref=uz.at[pl.ds(first, 2)], dst_ref=zrecv, send_sem=s_send.at[0], recv_sem=s_recv.at[0],
        device_id=(me_x, me_y, other_z), device_id_type=MESH)
    z_copy.start()

    has_l, has_r = me_x > 0, me_x < nx_dev - 1
    has_d, has_u = me_y > 0, me_y < ny_dev - 1
    for have, ref in ((has_l, xl), (has_r, xr), (has_d, yl), (has_u, yr)):
        @pl.when(jnp.logical_not(have))
        def _(ref=ref):
            ref[...] = jnp.zeros(ref.shape, F32)

    z_copy.wait()
    left_on = jnp.where(me_z == 1, 1.0, 0.0)
    right_on = 1.0 - left_on
    zl = zrecv[1] * left_on
    zr0, zr1 = zrecv[0] * right_on, zrecv[1] * right_on
    def zf(i, y):
        y = coef(0, 1, start_z + i) * y
        cz[i + 1] = uz[i] + y
        return y
    lax.fori_loop(0, dz, zf, zl, unroll=True)
    y = coef(0, 1, start_z + dz) * cz[dz]
    cz[dz + 1] = zr0 + y
    y = coef(0, 1, start_z + dz + 1) * y
    cz[dz + 2] = zr1 + y
    def zb(i, y):
        r = dz - 1 - i
        y = coef(0, 2, start_z + r) * y
        cz[r + 1] = cz[r + 1] + y
        return y
    y = lax.fori_loop(0, dz, zb, zr0, unroll=True)
    cz[0] = zl + coef(0, 2, start_z - 1) * (uz[0] + y)
    for i in range(dz + 3, zp):
        cz[i] = jnp.zeros((dx, dy), F32)
    for i in range(dx // 8):
        ce[HALO - 1 + 8 * i:HALO - 1 + 8 * i + 8] = jnp.swapaxes(cz[:, 8 * i:8 * i + 8, :], 0, 1)

    def xf(i, y):
        y = coef(1, 0, start_x + i) * ce[HALO - 1 + i] + coef(1, 1, start_x + i) * y
        ux[i] = y
        return y
    lax.fori_loop(0, dx, xf, jnp.zeros((zp, dy), F32), unroll=True)
    def xb(i, y):
        r = dx - 1 - i
        y = coef(1, 2, start_x + r) * y
        ux[r] = ux[r] + y
        return y + coef(1, 0, start_x + r) * ce[HALO - 1 + r]
    lax.fori_loop(0, dx, xb, jnp.zeros((zp, dy), F32), unroll=True)

    def pair(low_src, low_dst, high_src, high_dst, sem, low_id, high_id, low_ok, high_ok):
        low = pltpu.make_async_remote_copy(
            src_ref=low_src, dst_ref=low_dst, send_sem=s_send.at[sem], recv_sem=s_recv.at[sem],
            device_id=low_id, device_id_type=MESH)
        high = pltpu.make_async_remote_copy(
            src_ref=high_src, dst_ref=high_dst, send_sem=s_send.at[sem + 1], recv_sem=s_recv.at[sem + 1],
            device_id=high_id, device_id_type=MESH)
        @pl.when(low_ok)
        def _():
            low.start()
        @pl.when(high_ok)
        def _():
            high.start()
        def wait():
            @pl.when(low_ok)
            def _():
                low.wait_send()
                high.wait_recv()
            @pl.when(high_ok)
            def _():
                high.wait_send()
                low.wait_recv()
        return wait

    nch, nslot = zp // 8, dy // HALO
    rows = ex // nslot
    for i in range(dx + 2 * HALO - 1, ex):
        ce[i] = jnp.zeros((zp, dy), F32)
    waits_x, waits_y = [], []
    for c in range(nch):
        zs = pl.ds(8 * c, 8)
        waits_x.append(pair(
            ux.at[pl.ds(0, HALO), zs], xr.at[:, zs], ux.at[pl.ds(dx - HALO, HALO), zs], xl.at[:, zs],
            6 + 2 * c, (me_x - 1, me_y, me_z), (me_x + 1, me_y, me_z), has_l, has_r))

    tz, sz = taps_of(sub[0])
    tx, sx = taps_of(sub[1])
    ty, sy = taps_of(sub[2])
    lane = iota((1, dy), 1)
    group = lane // BRICK
    ox_v, oy_v = [], []
    for bx in range(nbx):
        vx = jnp.zeros((1, dy), jnp.int32)
        vy = jnp.zeros((1, dy), jnp.int32)
        for by in range(nby):
            vx = jnp.where(group == by, off[0, bx, by], vx)
            vy = jnp.where(group == by, off[1, bx, by], vy)
        ox_v.append(vx)
        oy_v.append(vy)

    nslot = dy // HALO
    col = iota((dy, 2 * dy), 1)
    src = iota((dy, 2 * dy), 0)
    lane_in = jnp.where(col < dy, col, col - dy)
    slot = lane_in // HALO
    at = lane_in - slot * HALO + jnp.where(col < dy, 0, dy - HALO)
    ends3[...] = stack3(jnp.where(slot == 0, inverse_entry(start_y + at, start_y + src, ny), 0.0))

    wide = 2 * dy
    jcol = iota((dy, wide), 1) - HALO
    jin = (start_y + jcol >= 0) & (start_y + jcol < ny) & (jcol < dy + HALO)
    own_part = jnp.where(jin, inverse_entry(
        jnp.clip(start_y + jcol, 0, ny - 1), start_y + iota((dy, wide), 0), ny), 0.0)
    m = iota((dy, wide), 0)
    jf = (start_y + jcol + 1).astype(F32)
    parity = 1.0 - 2.0 * (jcol & 1).astype(F32)
    t_left = (start_y * jnp.ones((1, 1), jnp.int32)).astype(F32)
    t_right = t_left + float(dy + 1)
    high = 1.0 - jnp.exp(-2.0 * LOG_POLE * (ny + 1 - jf))
    low = 1.0 - jnp.exp(-2.0 * LOG_POLE * jf)
    jown = jcol.astype(F32)
    from_left = -parity * jnp.exp(-LOG_POLE * (jown + 1.0)) * high / (
        1.0 - jnp.exp(-2.0 * LOG_POLE * (ny + 1 - t_left)))
    from_right = parity * jnp.exp(LOG_POLE * (jown - float(dy))) * low / (
        1.0 - jnp.exp(-2.0 * LOG_POLE * t_right))
    if dy % 2:
        from_right = -from_right
    left_col = jnp.where(jcol < 0, jnp.where(m - HALO == jcol, 1.0, 0.0),
                         jnp.where(m == HALO - 1, from_left, 0.0))
    right_col = jnp.where(jcol >= dy, jnp.where(m - HALO + dy == jcol, 1.0, 0.0),
                          jnp.where(m == HALO, from_right, 0.0))
    halo_part = jnp.where(m < HALO, left_col, jnp.where(m < 2 * HALO, right_col, 0.0))
    halo_part = jnp.where(jin, halo_part, 0.0)
    full_y = jnp.concatenate([own_part, halo_part], axis=0)
    for bx, wref in ((0, w0), (1, w1)):
        jrow = iota((wide, dy), 0) - HALO
        want = lane + oy_v[bx]
        ok_y = jnp.where((start_y + want >= 0) & (start_y + want < ny), 1.0, 0.0)
        picks = []
        for taps in (ty, sy):
            acc = jnp.zeros((wide, dy), F32)
            for c in range(4):
                acc = jnp.where(jrow == want + (c - 1), taps[c], acc)
            picks.append(acc * ok_y)
        wref[...] = stack3(jnp.dot(full_y, jnp.concatenate(picks, axis=1), precision=HIGHEST,
                                   preferred_element_type=F32))

    ones = jnp.where(iota((dy, dy), 0) // BRICK == iota((dy, dy), 1) // BRICK, 1.0, 0.0)
    half = float(dz * BRICK * BRICK)

    def group_sum(rows):
        return jnp.dot(rows, ones, precision=HIGHEST, preferred_element_type=F32)

    def row8(vecs):
        rows = iota((8, dy), 0)
        out = jnp.zeros((8, dy), F32)
        for i, v in enumerate(vecs):
            out = jnp.where(rows == i, v, out)
        return out

    load_fix.wait()
    for i in range(dx // 8):
        ft[8 * i:8 * i + 8] = jnp.swapaxes(fix[:, 8 * i:8 * i + 8, :], 0, 1)
    fsum = [jnp.sum(jnp.sum(ft[BRICK * b:BRICK * b + BRICK], axis=0), axis=0, keepdims=True) for b in range(nbx)]
    mean_f = group_sum(row8(fsum)) / half
    sff = []
    for b in range(nbx):
        cf = ft[BRICK * b:BRICK * b + BRICK] - mean_f[b:b + 1][None]
        ft[BRICK * b:BRICK * b + BRICK] = cf
        sff.append(jnp.sum(jnp.sum(cf * cf, axis=0), axis=0, keepdims=True))

    def combine(c):
        zs = pl.ds(8 * c, 8)
        def gf(i, y):
            y = coef(1, 1, start_x + i) * y
            ce[HALO - 1 + i, zs] = ux[i, zs] + y
            return y
        lax.fori_loop(0, dx, gf, xl[HALO - 1, zs], unroll=True)
        def gr(i, y):
            y = coef(1, 1, start_x + dx + i) * y
            ce[HALO - 1 + dx + i, zs] = xr[i, zs] + y
            return y
        lax.fori_loop(0, HALO, gr, ce[HALO - 1 + dx - 1, zs], unroll=True)
        def gb(i, y):
            r = dx - 1 - i
            y = coef(1, 2, start_x + r) * y
            ce[HALO - 1 + r, zs] = ce[HALO - 1 + r, zs] + y
            return y
        y = lax.fori_loop(0, dx, gb, xr[0, zs], unroll=True)
        def gl(i, y):
            y = coef(1, 2, start_x - 1 - i) * y
            ce[HALO - 2 - i, zs] = xl[HALO - 1 - i, zs] + y
            return y
        lax.fori_loop(0, HALO - 1, gl, ux[0, zs] + y, unroll=True)

    n8 = rows * 8
    def pack(c):
        res = split3(ce[:, 8 * c:8 * c + 8, :].reshape(ex * 8, dy), ends3[...])
        low, high = None, None
        for k in range(nslot):
            a = res[n8 * k:n8 * k + n8, :dy]
            b = res[n8 * k:n8 * k + n8, dy:]
            if k > 0:
                a = pltpu.roll(a, HALO * k, 1)
                b = pltpu.roll(b, HALO * k, 1)
            low = a if low is None else low + a
            high = b if high is None else high + b
        packl[c] = low.reshape(rows, 8, dy)
        packr[c] = high.reshape(rows, 8, dy)

    lane3 = iota((n8, dy), 1)
    def spread_y(c):
        left = yl[c].reshape(n8, dy)
        right = yr[c].reshape(n8, dy)
        halos = []
        for k in range(nslot):
            a, b = left, right
            if k > 0:
                a = pltpu.roll(a, dy - HALO * k, 1)
            if k != 1:
                b = pltpu.roll(b, (dy + HALO - HALO * k) % dy, 1)
            halos.append(jnp.where(lane3 < HALO, a, jnp.where(lane3 < 2 * HALO, b, 0.0)))
        own = ce[:, 8 * c:8 * c + 8, :].reshape(ex * 8, dy)
        both = jnp.concatenate([own, jnp.concatenate(halos, axis=0)], axis=1)
        count = (ex - rows) * 8
        g0[:, 8 * c:8 * c + 8, :] = split3(both[:count], w0[...]).reshape(ex - rows, 8, 2 * dy)
        g1[:, 8 * c:8 * c + 8, :] = split3(both[n8:], w1[...]).reshape(ex - rows, 8, 2 * dy)

    for c in range(nch):
        waits_x[c]()
        combine(c)
        pack(c)
        waits_y.append(pair(packl.at[c], yr.at[c], packr.at[c], yl.at[c], 6 + 2 * nch + 2 * c,
                            (me_x, me_y - 1, me_z), (me_x, me_y + 1, me_z), has_d, has_u))
        if c > 0:
            waits_y[c - 1]()
            spread_y(c - 1)
    waits_y[nch - 1]()
    spread_y(nch - 1)

    group2 = jnp.concatenate([group, group], axis=1)
    wsum = []
    for bx, gref in ((0, g0), (1, g1)):
        base = [off[0, bx, by] + RANGE + bx * (BRICK - rows) for by in range(nby)]
        def pick(i, c, gref=gref, base=base):
            v = gref[base[0] + i]
            for by in range(1, nby):
                v = jnp.where(group2 == by, gref[base[by] + i], v)
            hs[i] = v
            return c
        lax.fori_loop(0, BRICK + 3, pick, 0)
        def fir(i, total, bx=bx):
            gx_pos = start_x + bx * BRICK + i + ox_v[bx]
            ok_x = jnp.where((gx_pos >= 0) & (gx_pos < nx), 1.0, 0.0)
            h = [hs[i + c] for c in range(4)]
            hv = [v[:, :dy] for v in h]
            hd = [v[:, dy:] for v in h]
            def comb(w, vs):
                return (w[0] * vs[0] + w[1] * vs[1] + w[2] * vs[2] + w[3] * vs[3]) * ok_x
            val, dxx, dyy = comb(tx, hv), comb(sx, hv), comb(tx, hd)
            def zfir(w, v):
                return w[0] * v[0:dz] + w[1] * v[1:dz + 1] + w[2] * v[2:dz + 2] + w[3] * v[3:dz + 3]
            out = zfir(tz, val)
            r = bx * BRICK + i
            wv[r] = out
            px[r] = zfir(tz, dxx)
            py[r] = zfir(tz, dyy)
            pz[r] = zfir(sz, val)
            return total + out
        total = lax.fori_loop(0, BRICK, fir, jnp.zeros((dz, dy), F32))
        wsum.append(jnp.sum(total, axis=0, keepdims=True))

    mean_w = group_sum(row8(wsum)) / half
    sww, sfw = [], []
    for b in range(nbx):
        cw = wv[BRICK * b:BRICK * b + BRICK] - mean_w[b:b + 1][None]
        wv[BRICK * b:BRICK * b + BRICK] = cw
        cf = ft[BRICK * b:BRICK * b + BRICK]
        sww.append(jnp.sum(jnp.sum(cw * cw, axis=0), axis=0, keepdims=True))
        sfw.append(jnp.sum(jnp.sum(cf * cw, axis=0), axis=0, keepdims=True))
    sums = group_sum(row8(sff + sww + sfw))
    stat[0] = row8([mean_f[b:b + 1] for b in range(nbx)] + [mean_w[b:b + 1] for b in range(nbx)])
    stat[1] = sums
    st_copy = pltpu.make_async_remote_copy(
        src_ref=stat, dst_ref=statr, send_sem=s_send.at[5], recv_sem=s_recv.at[5],
        device_id=(me_x, me_y, other_z), device_id_type=MESH)
    st_copy.start()

    ne = nbx + 4
    xrow = [[0.0] * dx for _ in range(ne)]
    for e in range(ne):
        for r in range(dx):
            u = abs(r - BRICK * (e - 2) - BRICK // 2) / BRICK
            xrow[e][r] = (2.0 / 3.0 - u * u + u ** 3 / 2.0) if u < 1 else max(2.0 - u, 0.0) ** 3 / 6.0
    for d, pref in enumerate((px, py, pz)):
        for b in range(nbx):
            for kind, other in enumerate((ft, wv, None)):
                accs = [None] * 5
                for r in range(BRICK * b, BRICK * b + BRICK):
                    force = pref[r] if other is None else pref[r] * other[r]
                    for e in range(5):
                        if xrow[b + e][r] != 0.0:
                            t = xrow[b + e][r] * force
                            accs[e] = t if accs[e] is None else accs[e] + t
                for e in range(5):
                    proj[((d * nbx + b) * 3 + kind) * 5 + e] = accs[e]
    st_copy.wait()
    voxels = 2.0 * half
    alphas, betas, gammas, nccs = [], [], [], []
    own_m, oth_m = stat[0], statr[0]
    own_s, oth_s = stat[1], statr[1]
    diff = own_m - oth_m
    for b in range(nbx):
        df, dw = diff[b:b + 1], diff[nbx + b:nbx + b + 1]
        def both_halves(i, extra):
            return own_s[i:i + 1] + oth_s[i:i + 1] + extra * (half / 2.0)
        ff = both_halves(b, df * df)
        ww = both_halves(nbx + b, dw * dw)
        fw = both_halves(2 * nbx + b, df * dw)
        inv = lax.rsqrt(ff * ww + EPSILON)
        ratio = fw / (ww + EPSILON)
        nccs.append(fw * inv)
        alphas.append(voxels * inv)
        betas.append(ratio)
        gammas.append(0.5 * (df - ratio * dw))
    every = jnp.where(iota((dy, dy), 0) == BRICK * iota((dy, dy), 1), 1.0, 0.0)
    ncc_rows = jnp.dot(row8(nccs), every, precision=HIGHEST, preferred_element_type=F32)
    ncc_out[...] = ncc_rows[:nbx, :nby]

    zrow = (start_z + iota((dz, 1), 0)).astype(F32)
    bz = [bspline((zrow - float(BRICK * k + BRICK // 2)) / BRICK) for k in range(nz // BRICK)]
    nk = nz // BRICK
    ycol = iota((dy, dy), 1)
    yoff = (iota((dy, dy), 0) - BRICK * (ycol - 2) - BRICK // 2).astype(F32) / BRICK
    by_mat = jnp.where(ycol < nby + 4, bspline(yoff), 0.0)
    for d in range(3):
        accs = [None] * ne
        for b in range(nbx):
            for e in range(5):
                at3 = ((d * nbx + b) * 3) * 5 + e
                t = alphas[b] * (proj[at3] - betas[b] * proj[at3 + 5] + gammas[b] * proj[at3 + 10])
                accs[b + e] = t if accs[b + e] is None else accs[b + e] + t
        for e in range(ne):
            for k in range(nk):
                row = e * 3 * nk + d * nk + k
                part[row:row + 1, :] = jnp.sum(accs[e] * bz[k], axis=0, keepdims=True)
    full = jnp.dot(part[...], by_mat, precision=HIGHEST, preferred_element_type=F32) * (1.0 / SUPPORT_NORM)
    tiles = nbx * 3 * nk // 8
    for ix in range(3):
        first_row = (0, 2, nbx + 2)[ix] * 3 * nk
        tile = None
        for g in range(tiles):
            t = full[first_row + 8 * g:first_row + 8 * g + 8]
            t = t if g == 0 else pltpu.roll(t, 16 * g, 1)
            tile = t if tile is None else tile + t
        out_tiles[ix] = tile

    def slot_of(ix, iy, iz):
        return ((ix + 1) * 3 + (iy + 1)) * 2 + iz

    for ix, iy, iz, ok, target in peers:
        there = slot_of(-ix, -iy, iz)
        here = slot_of(ix, iy, iz)
        @pl.when(jnp.logical_not(ok))
        def _(here=here):
            gather[here] = jnp.zeros(gather.shape[1:], F32)
        @pl.when(ok)
        def _(ix=ix, there=there, target=target):
            pltpu.make_async_remote_copy(
                src_ref=out_tiles.at[ix + 1],
                dst_ref=gather.at[there], send_sem=f_send.at[there], recv_sem=f_recv.at[there],
                device_id=target, device_id_type=MESH).start()
    for ix, iy, iz, ok, target in peers:
        there = slot_of(-ix, -iy, iz)
        here = slot_of(ix, iy, iz)
        @pl.when(ok)
        def _(ix=ix, there=there, here=here, target=target):
            pltpu.make_async_remote_copy(
                src_ref=out_tiles.at[ix + 1],
                dst_ref=gather.at[there], send_sem=f_send.at[there], recv_sem=f_recv.at[there],
                device_id=target, device_id_type=MESH).wait_send()
            pltpu.make_async_remote_copy(
                src_ref=out_tiles.at[0],
                dst_ref=gather.at[here], send_sem=f_send.at[here], recv_sem=f_recv.at[here],
                device_id=target, device_id_type=MESH).wait_recv()
    gather_own = out_tiles[1]
    lane_c = iota((8, dy), 1) & 15
    result = None
    for iy in (-1, 0, 1):
        total = gather_own if iy == 0 else None
        for ix in (-1, 0, 1):
            for iz in (0, 1):
                if (ix, iy, iz) == (0, 0, 0):
                    continue
                v = gather[slot_of(ix, iy, iz)]
                total = v if total is None else total + v
        if iy == 0:
            moved = pltpu.roll(total, dy - 2, 1)
        elif iy < 0:
            moved = jnp.where(lane_c < 2, pltpu.roll(total, dy - (nby + 2), 1), 0.0)
        else:
            moved = jnp.where(lane_c >= nby - 2, pltpu.roll(total, nby - 2, 1), 0.0)
        result = moved if result is None else result + moved
    for g in range(tiles):
        t = result if g == 0 else pltpu.roll(result, dy - 16 * g, 1)
        for q in range(8):
            i, rest = divmod(8 * g + q, 3 * nk)
            d, k = divmod(rest, nk)
            grad_out[d, k, i:i + 1, :] = t[q:q + 1, :nby]


def shards(sizes, moving_image, fixed_image, subvoxel, brick_offset):
    nx_dev, ny_dev, nz_dev = sizes
    dz, dx, dy = moving_image.shape
    nz, nx, ny = dz * nz_dev, dx * nx_dev, dy * ny_dev
    table, width_t = factor_tables((nz, nx, ny))
    zp = -(-(dz + 3) // 8) * 8
    nslot = dy // HALO
    ex = -(-(dx + 2 * HALO - 1) // nslot) * nslot
    rows = ex // nslot
    nch = zp // 8
    nbx, nby, nk = dx // BRICK, dy // BRICK, nz // BRICK
    cfg = (nx_dev, ny_dev, width_t, nz, nx, ny, dz, dx, dy, zp, ex)
    vm = lambda *shape: pltpu.VMEM(shape, F32)
    vspec = pl.BlockSpec(memory_space=pltpu.VMEM)
    hspec = pl.BlockSpec(memory_space=pl.ANY)
    sspec = pl.BlockSpec(memory_space=pltpu.SMEM)
    return pl.pallas_call(
        functools.partial(kernel, cfg),
        out_shape=(
            jax.ShapeDtypeStruct((nbx, nby), F32),
            jax.ShapeDtypeStruct((3, nk, nbx, nby), F32),
        ),
        in_specs=[sspec, sspec, sspec, hspec, hspec],
        out_specs=(vspec, vspec),
        scratch_shapes=[
            vm(dz, dx, dy), vm(dz, dx, dy), pltpu.SemaphoreType.DMA((2,)),
            vm(dz, dx, dy), vm(2, dx, dy), vm(zp, dx, dy),
            vm(dx, zp, dy), vm(HALO, zp, dy), vm(HALO, zp, dy), vm(ex, zp, dy),
            vm(nch, rows, 8, dy), vm(nch, rows, 8, dy), vm(nch, rows, 8, dy), vm(nch, rows, 8, dy),
            pltpu.VMEM((3 * dy, 2 * dy), BF16),
            pltpu.VMEM((6 * dy, 2 * dy), BF16), pltpu.VMEM((6 * dy, 2 * dy), BF16),
            vm(ex - rows, zp, 2 * dy), vm(ex - rows, zp, 2 * dy), vm(BRICK + 3, zp, 2 * dy),
            vm(dx, dz, dy), vm(dx, dz, dy), vm(dx, dz, dy), vm(dx, dz, dy), vm(dx, dz, dy),
            vm(3 * nbx * 3 * 5, dz, dy),
            vm(2, 8, dy), vm(2, 8, dy),
            vm((nbx + 4) * 3 * nk, dy), vm(3, 8, dy), vm(18, 8, dy),
            pltpu.SemaphoreType.DMA((6 + 4 * nch,)), pltpu.SemaphoreType.DMA((6 + 4 * nch,)),
            pltpu.SemaphoreType.DMA((18,)), pltpu.SemaphoreType.DMA((18,)),
        ],
        compiler_params=pltpu.CompilerParams(
            collective_id=0, has_side_effects=True, vmem_limit_bytes=56 * 1024 * 1024),
    )(jnp.asarray(table), subvoxel, brick_offset, moving_image, fixed_image)


def solution(mesh):
    sizes = (mesh.shape["gx"], mesh.shape["gy"], mesh.shape["gz"])
    return jax.shard_map(
        functools.partial(shards, sizes),
        mesh=mesh,
        in_specs=(P("gz", "gx", "gy"), P("gz", "gx", "gy"), P(), P(None, "gx", "gy")),
        out_specs=(P("gx", "gy"), P(None, None, "gx", "gy")),
        check_vma=False,
    )
```
